32 devices in a mesh: ctx: 4 (over x, core), chan: 8 (over z, y).
Axes of the slice: x: 2, y: 2, z: 4, core: 2. Of those that a mesh axis runs over, the one named last changes fastest.
Arguments:
- proj: bfloat16 [3, 1024, 4096], P(None, 'chan', 'ctx'), may hold values from -6 to 6
- taps: bfloat16 [3, 64, 128], replicated, may hold values from -0.5 to 0.5
- rate: float32 [1024, 16], P('chan'), may hold values from 0.00012207031 to 0.0333333333
- residue: float32 [1024, 16], P('chan'), may hold values from -6 to 6
- skip: float32 [1024], P('chan'), may hold values from -6 to 6
- out_weight: bfloat16 [1024, 1024], replicated, may hold values from -0.1875 to 0.1875
Outputs:
- output: bfloat16 [1024, 4096], P('chan', 'ctx')
The draws below stay inside these ranges and needn't reach their ends.
All inputs are finite; a program needn't handle non-finite values.
Results may differ from the reference program's by a relative error of at most 0.005.
Values may be sent and summed in bfloat16 or wider, within the bound.
A program may use at most 128 MiB of HBM per device.

```python
import math
import jax
import jax.numpy as jnp
from jax import lax

C = 1024
M = 16
GROUP = 16
TAPS = 128
LENGTH = 4096


def draw_rate(key, part):
    uniform_draw = jax.random.uniform(key, (C, M), jnp.float32)
    log_lowest = jnp.log(0.5 / LENGTH)
    return jnp.exp(log_lowest + (jnp.log(1.0 / 30.0) - log_lowest) * uniform_draw)


def level_of(key, dims, shards, least, largest):
    factor_of, own = 1.0, jax.random.fold_in(key, 6)
    for axis_at, parts in shards:
        steps = jnp.exp(jax.random.uniform(jax.random.fold_in(own, axis_at), (parts,), jnp.float32, least / len(shards), largest / len(shards)))
        factor_of = factor_of * jnp.repeat(steps, dims[axis_at] // parts).reshape([-1 if axis == axis_at else 1 for axis in range(len(dims))])
    return factor_of


def bell_draw(rng, shape, spread, bound, split=(), dtype=jnp.bfloat16):
    drawn = spread * jax.random.normal(rng, shape, jnp.float32)
    if split:
        drawn = drawn * level_of(rng, shape, split, -0.22, 0.18)
    return jnp.clip(drawn, -bound, bound).astype(dtype)


def setup_inputs(seed: int = 0) -> dict:
    key_of = jax.random.split(jax.random.key(seed), 7)
    proj = bell_draw(key_of[0], (3, C, LENGTH), 1.0, 6.0, ((1, 8), (2, 4)))
    taps = bell_draw(key_of[1], (3, C // GROUP, TAPS), TAPS ** -0.5, 0.5)
    rate = draw_rate(jax.random.fold_in(key_of[6], 71), 0)
    residue = bell_draw(key_of[3], (C, M), 1.0, 6.0, ((0, 8),), jnp.float32)
    skip = bell_draw(key_of[4], (C,), 1.0, 6.0, ((0, 8),), jnp.float32)
    out_weight = bell_draw(key_of[5], (C, C), C ** -0.5, 0.1875)
    return {"proj": proj, "taps": taps, "rate": rate, "residue": residue, "skip": skip, "out_weight": out_weight}


def reference(proj, taps, rate, residue, skip, out_weight):
    padded = jnp.pad(proj.astype(jnp.float32), ((0, 0), (0, 0), (TAPS - 1, 0)))
    kernel = jnp.repeat(taps.astype(jnp.float32), GROUP, axis=1)

    def add_tap(index, running):
        window = lax.dynamic_slice_in_dim(padded, (TAPS - 1 - index).astype(jnp.int32), LENGTH, 2)
        weight = lax.dynamic_slice_in_dim(kernel, index.astype(jnp.int32), 1, 2)
        return running + weight * window
    shorted = lax.fori_loop(0, TAPS, add_tap, jnp.zeros((3, C, LENGTH), jnp.float32))
    query_side = shorted[0]
    mixed = shorted[1] * shorted[2]
    residue_eff = residue * jnp.sqrt(2.0 * rate / M)
    positions = jnp.arange(LENGTH).astype(jnp.float32)
    group_size = math.gcd(C, 64)
    fft_len = 2 * LENGTH

    def one_group(packed):
        rate_group, residue_group, signal = packed
        filters = lax.optimization_barrier(jnp.sum(residue_group[:, :, None] * jnp.exp(-rate_group[:, :, None] * positions[None, None, :]), axis=1))
        product = jnp.fft.rfft(signal, n=fft_len) * jnp.fft.rfft(filters, n=fft_len)
        return jnp.fft.irfft(product, n=fft_len)[:, :LENGTH]
    longconv = lax.map(one_group, (rate.reshape(C // group_size, group_size, M), residue_eff.reshape(C // group_size, group_size, M), mixed.reshape(C // group_size, group_size, LENGTH))).reshape(C, LENGTH)
    gated = (query_side * (longconv + skip[:, None] * mixed)).astype(jnp.bfloat16)
    return jnp.dot(out_weight.T, gated, preferred_element_type=jnp.float32).astype(jnp.bfloat16)
```

```python
import functools
import jax
import jax.numpy as jnp
from jax import lax
from jax.experimental import pallas as pl
from jax.experimental.pallas import tpu as pltpu
from jax.sharding import PartitionSpec as P

GROUP = 16
BLOCK = 128
PIECES = 4
MESH = pl.DeviceIdType.MESH
HIGHEST = lax.Precision.HIGHEST


def iota(shape, axis):
    return lax.broadcasted_iota(jnp.int32, shape, axis)


def one_hot(hit, dtype=jnp.float32):
    return hit.astype(jnp.float32).astype(dtype)


def ring_place(chan, n):
    row, side = chan // 2, chan % 2
    return row + side * (n - 1 - 2 * row)


def ring_chan(place, n):
    side = place // (n // 2)
    row = place + side * (n - 1 - 2 * place)
    return 2 * row + side


def turned_tiles(work, groups, blocks, put):
    for g in range(groups):
        turned = work[pl.ds(g, BLOCK, stride=groups), :].astype(jnp.bfloat16).T
        for b in range(blocks):
            put(g, b, turned[b * GROUP : (b + 1) * GROUP])


def exchange(
    chans,
    chan,
    work,
    gath,
    weight,
    weight_copy,
    out_ref,
    parts,
    turned_weight,
    results,
    there_send,
    there_recv,
    back_send,
    back_recv,
):
    width = out_ref.shape[0]
    groups = width // GROUP

    def put(g, b, tile):
        parts[b, g * GROUP : (g + 1) * GROUP, :] = tile

    turned_tiles(work, groups, chans, put)
    order = sorted(range(1, chans), key=lambda hop: -min(hop, chans - hop))
    there, back = {}, {}
    for hop in order:
        peer = (chan + hop) % chans
        there[hop] = pltpu.make_async_remote_copy(
            src_ref=parts.at[peer],
            dst_ref=gath.at[chan],
            send_sem=there_send.at[hop - 1],
            recv_sem=there_recv.at[hop - 1],
            device_id={"chan": peer},
            device_id_type=MESH,
        )
        there[hop].start()
    gath[chan] = parts[chan]
    weight_copy.wait()
    turned_weight[...] = weight[...].T
    for hop in order:
        there[hop].wait_recv()
    everything = gath[...].reshape(chans * width, BLOCK)

    def project(shard):
        rows_of = pl.ds(pl.multiple_of(shard * width, width), width)
        return jnp.dot(
            turned_weight[rows_of, :], everything, preferred_element_type=jnp.float32
        ).astype(jnp.bfloat16)

    own_columns = pl.ds(pl.multiple_of(chan * BLOCK, BLOCK), BLOCK)
    for hop in order:
        peer = (chan + hop) % chans
        results[hop - 1] = project(peer)
        back[hop] = pltpu.make_async_remote_copy(
            src_ref=results.at[hop - 1],
            dst_ref=out_ref.at[:, own_columns],
            send_sem=back_send.at[hop - 1],
            recv_sem=back_recv.at[hop - 1],
            device_id={"chan": peer},
            device_id_type=MESH,
        )
        back[hop].start()
    out_ref[:, own_columns] = project(chan)
    for hop in order:
        back[hop].wait_recv()
    for hop in order:
        there[hop].wait_send()
        back[hop].wait_send()


def ring(
    chans,
    chan,
    place,
    left,
    right,
    work,
    gath,
    own_weight,
    weight_copy,
    out_ref,
    acc,
    ring_send,
    ring_recv,
):
    width, tokens = out_ref.shape
    groups, blocks = width // GROUP, tokens // BLOCK
    cols = tokens // PIECES
    per_piece = blocks // PIECES

    def put(g, b, tile):
        inside = (b % per_piece) * BLOCK
        gath[
            chan, b // per_piece, g * GROUP : (g + 1) * GROUP, inside : inside + BLOCK
        ] = tile

    turned_tiles(work, groups, blocks, put)
    half = chans // 2

    def ring_copy(way, hop, piece):
        shard = ring_chan((place + chans + (-hop if way == 0 else hop)) % chans, chans)
        return pltpu.make_async_remote_copy(
            src_ref=gath.at[shard, piece],
            dst_ref=gath.at[shard, piece],
            send_sem=ring_send.at[way, hop, piece],
            recv_sem=ring_recv.at[way, hop, piece],
            device_id={"chan": right if way == 0 else left},
            device_id_type=MESH,
        )

    def travels(way, hop, piece):
        if hop < half - 1:
            return True
        return hop == half - 1 and (piece < PIECES // 2) == (way == 0)

    copies = {}
    for piece in range(PIECES):
        for way in range(2):
            copies[way, 0, piece] = ring_copy(way, 0, piece)
            copies[way, 0, piece].start()
    weight_copy.wait()

    def project(shard, piece):
        rows_of = pl.ds(pl.multiple_of(shard * width, width), width)
        return lax.dot_general(
            own_weight[rows_of, :],
            gath[shard, piece],
            (((0,), (0,)), ((), ())),
            preferred_element_type=jnp.float32,
        )

    for piece in range(PIECES):
        acc[piece] = project(chan, piece)
    for hop in range(1, half + 1):
        for piece in range(PIECES):
            arrived = []
            for way in range(2):
                if not travels(way, hop - 1, piece):
                    continue
                copies[way, hop - 1, piece].wait_recv()
                if travels(way, hop, piece):
                    copies[way, hop, piece] = ring_copy(way, hop, piece)
                    copies[way, hop, piece].start()
                arrived.append(
                    ring_chan((place + chans + (-hop if way == 0 else hop)) % chans, chans)
                )
            total = acc[piece]
            for shard in arrived:
                total = total + project(shard, piece)
            if hop == half:
                out_ref[:, piece * cols : (piece + 1) * cols] = total.astype(out_ref.dtype)
            else:
                acc[piece] = total

    for key in copies:
        copies[key].wait_send()


def is_swap(chans, width, tokens):
    return chans > 1 and width == BLOCK and tokens == chans * BLOCK


def fused(
    ctx,
    chans,
    proj_in,
    taps_in,
    rate_in,
    residue_in,
    skip_in,
    weight_ref,
    out_ref,
    proj_ref,
    taps_ref,
    rate_ref,
    residue_ref,
    skip_ref,
    halo,
    query,
    mixed,
    work,
    bands,
    rate_s,
    residue_s,
    state,
    ends,
    own_weight,
    gath,
    weight_sem,
    load_sems,
    halo_sems,
    end_send,
    end_recv,
    *rest,
):
    width, tokens = proj_ref.shape[1:]
    modes = rate_ref.shape[0]
    groups, blocks = width // GROUP, tokens // BLOCK
    lanes = blocks * GROUP
    swap = is_swap(chans, width, tokens)
    index = lax.axis_index("ctx")
    chan = lax.axis_index("chan")
    if swap:
        peers = [(chan + hop) % chans for hop in range(1, chans)]
    else:
        place = ring_place(chan, chans)
        right = ring_chan((place + 1) % chans, chans)
        left = ring_chan((place + chans - 1) % chans, chans)
        peers = [left, right]

    barrier = pltpu.get_barrier_semaphore()
    for hop in range(1, ctx):
        pl.semaphore_signal(
            barrier, inc=1, device_id={"ctx": (index + hop) % ctx}, device_id_type=MESH
        )
    for peer in peers:
        pl.semaphore_signal(barrier, inc=1, device_id={"chan": peer}, device_id_type=MESH)

    loads = [
        pltpu.make_async_copy(source, target, load_sems.at[k])
        for k, (source, target) in enumerate(
            (
                (taps_in, taps_ref),
                (rate_in, rate_ref),
                (residue_in, residue_ref),
                (skip_in, skip_ref),
                (proj_in, proj_ref),
            )
        )
    ]
    for load in loads:
        load.start()
    if swap or weight_ref.shape[1] == width:
        weight_from = weight_ref
    else:
        weight_from = weight_ref.at[:, pl.ds(pl.multiple_of(chan * width, width), width)]
    weight_copy = pltpu.make_async_copy(weight_from, own_weight, weight_sem)
    weight_copy.start()

    pl.semaphore_wait(barrier, ctx - 1 + len(peers))
    halo_copy = pltpu.make_async_remote_copy(
        src_ref=proj_in.at[:, :, pl.ds(tokens - BLOCK, BLOCK)],
        dst_ref=halo,
        send_sem=halo_sems.at[0],
        recv_sem=halo_sems.at[1],
        device_id={"ctx": (index + 1) % ctx},
        device_id_type=MESH,
    )

    @pl.when(index < ctx - 1)
    def _():
        halo_copy.start()

    loads[0].wait()
    all_groups = taps_ref.shape[1]
    pick = one_hot(
        iota((groups, all_groups), 1) == iota((groups, all_groups), 0) + chan * groups,
        jnp.bfloat16,
    )
    flip = one_hot(
        iota((BLOCK, 2 * BLOCK), 1) == BLOCK - iota((BLOCK, 2 * BLOCK), 0), jnp.bfloat16
    )
    def make_bands(stream):
        own = jnp.dot(pick, taps_ref[stream], preferred_element_type=jnp.float32)
        rows = jnp.dot(own.astype(jnp.bfloat16), flip, preferred_element_type=jnp.float32)
        for g in range(groups):
            wide = jnp.broadcast_to(rows[g : g + 1, :], (BLOCK, 2 * BLOCK))
            bands[stream, g] = pltpu.roll(wide, 0, 1, stride=1, stride_axis=0).astype(
                jnp.bfloat16
            )

    make_bands(1)
    make_bands(2)
    loads[1].wait()
    high = modes * groups
    expand = one_hot(iota((high, modes), 0) // groups == iota((high, modes), 1))
    kept = iota((high, width), 1) // GROUP == iota((high, width), 0) % groups
    spread = one_hot(iota((width, lanes), 0) % GROUP == iota((width, lanes), 1) % GROUP)

    def spread_rows(value):
        tall = lax.dot_general(
            expand,
            value,
            (((1,), (0,)), ((), ())),
            precision=HIGHEST,
            preferred_element_type=jnp.float32,
        )
        return jnp.dot(
            jnp.where(kept, tall, 0.0),
            spread,
            precision=HIGHEST,
            preferred_element_type=jnp.float32,
        )

    rate_s[...] = spread_rows(rate_ref[...])

    def of_mode(ref, m):
        return ref[m * groups : (m + 1) * groups, :]

    decay = [jnp.exp(-of_mode(rate_s, m)) for m in range(modes)]

    loads[4].wait()

    @pl.when(index > 0)
    def _():
        halo_copy.wait_recv()

    @pl.when(index == 0)
    def _():
        halo[...] = jnp.zeros_like(halo)

    def short(stream, g):
        rows_of = slice(g * GROUP, (g + 1) * GROUP)
        tiles = [proj_ref[stream, rows_of, b * BLOCK : (b + 1) * BLOCK] for b in range(blocks)]
        before = [halo[stream, rows_of, :]] + tiles[:-1]
        signal = jnp.concatenate(
            [jnp.concatenate(before, axis=0), jnp.concatenate(tiles, axis=0)], axis=1
        )
        return lax.dot_general(
            bands[stream, g], signal, (((1,), (1,)), ((), ())), preferred_element_type=jnp.float32
        )

    for g in range(groups):
        mixed[pl.ds(g, BLOCK, stride=groups), :] = short(1, g) * short(2, g)

    def gather_step(r, states):
        x = mixed[pl.ds(pl.multiple_of(r * groups, groups), groups), :]
        return tuple(d * s + x for d, s in zip(decay, states))

    zero = jnp.zeros((groups, lanes), jnp.float32)
    last = lax.fori_loop(0, BLOCK, gather_step, (zero,) * modes, unroll=16)
    at = iota(zero.shape, 1) // GROUP
    for m in range(modes):
        total, hop = last[m], 1
        while hop < blocks:
            moved = jnp.exp(of_mode(rate_s, m) * (-float(BLOCK * hop))) * pltpu.roll(
                total, GROUP * hop, 1
            )
            total = total + jnp.where(at >= hop, moved, 0.0)
            hop *= 2
        state[m * groups : (m + 1) * groups, :] = total

    end_copies = [
        pltpu.make_async_remote_copy(
            src_ref=state,
            dst_ref=ends.at[hop - 1],
            send_sem=end_send.at[hop - 1],
            recv_sem=end_recv.at[hop - 1],
            device_id={"ctx": (index + hop) % ctx},
            device_id_type=MESH,
        )
        for hop in range(1, ctx)
    ]
    for hop in range(1, ctx):

        @pl.when(index < ctx - hop)
        def _():
            end_copies[hop - 1].start()

    make_bands(0)
    for g in range(groups):
        query[pl.ds(g, BLOCK, stride=groups), :] = short(0, g)
    loads[2].wait()
    loads[3].wait()
    residue_s[...] = spread_rows(residue_ref[...]) * jnp.sqrt(2.0 * rate_s[...] / modes)
    skip_rows = jnp.where(
        iota((groups, width), 1) // GROUP == iota((groups, width), 0),
        jnp.broadcast_to(skip_ref[...], (groups, width)),
        0.0,
    )
    skip = jnp.dot(skip_rows, spread, precision=HIGHEST, preferred_element_type=jnp.float32)
    at_tokens = at.astype(jnp.float32) * float(BLOCK)
    across = [jnp.exp(of_mode(rate_s, m) * (-float(tokens))) for m in range(modes)]
    shift = [jnp.exp(-of_mode(rate_s, m) * at_tokens) for m in range(modes)]

    for hop in range(1, ctx):

        @pl.when(index >= hop)
        def _():
            end_copies[hop - 1].wait_recv()

        @pl.when(index < hop)
        def _():
            ends[hop - 1] = jnp.zeros((high, lanes), jnp.float32)

    entry, weight = [], []
    for m in range(modes):
        incoming = jnp.zeros_like(zero)
        for hop in range(ctx - 1, 0, -1):
            incoming = across[m] * incoming + ends[hop - 1, m * groups : (m + 1) * groups, :]
        incoming = jnp.where(at == blocks - 1, incoming, 0.0)
        hop = 1
        while hop < blocks:
            incoming = incoming + pltpu.roll(incoming, GROUP * hop, 1)
            hop *= 2
        own = jnp.where(at >= 1, pltpu.roll(of_mode(state, m), GROUP, 1), 0.0)
        entry.append(own + shift[m] * incoming)
        weight.append(of_mode(residue_s, m))

    def step(r, states):
        where = pl.ds(pl.multiple_of(r * groups, groups), groups)
        x = mixed[where, :]
        new = tuple(d * s + x for d, s in zip(decay, states))
        parts = [w * s for w, s in zip(weight, new)] + [skip * x]
        while len(parts) > 1:
            parts = [a + b for a, b in zip(parts[::2], parts[1::2])] + (
                [parts[-1]] if len(parts) % 2 else []
            )
        work[where, :] = query[where, :] * parts[0]
        return new

    lax.fori_loop(0, BLOCK, step, tuple(entry), unroll=8)
    if swap:
        exchange(chans, chan, work, gath, own_weight, weight_copy, out_ref, *rest)
    else:
        ring(chans, chan, place, left, right, work, gath, own_weight, weight_copy, out_ref, *rest)

    @pl.when(index < ctx - 1)
    def _():
        halo_copy.wait_send()

    for hop in range(1, ctx):

        @pl.when(index < ctx - hop)
        def _():
            end_copies[hop - 1].wait_send()


def per_device(ctx, chans, proj, taps, rate, residue, skip, out_weight):
    width, tokens = proj.shape[1:]
    modes = rate.shape[1]
    groups, blocks = width // GROUP, tokens // BLOCK
    lanes = blocks * GROUP
    swap = is_swap(chans, width, tokens)
    if width % 128:
        out_weight = lax.dynamic_slice_in_dim(
            out_weight, lax.axis_index("chan") * width, width, 1
        )
    vmem = pl.BlockSpec(memory_space=pltpu.VMEM)
    if swap:
        blocks_of = pltpu.VMEM((chans, width, BLOCK), jnp.bfloat16)
        square = pltpu.VMEM(out_weight.shape, jnp.bfloat16)
        several = pltpu.SemaphoreType.DMA((chans - 1,))
        weight_scratch, gath_scratch = square, blocks_of
        rest = [blocks_of, square, blocks_of] + [several] * 4
    else:
        weight_scratch = pltpu.VMEM((chans * width, width), jnp.bfloat16)
        gath_scratch = pltpu.VMEM((chans, PIECES, width, tokens // PIECES), jnp.bfloat16)
        hops = pltpu.SemaphoreType.DMA((2, chans // 2, PIECES))
        rest = [pltpu.VMEM((PIECES, width, tokens // PIECES), jnp.float32), hops, hops]
    major = pltpu.VMEM((BLOCK * groups, lanes), jnp.float32)
    table = pltpu.VMEM((modes * groups, lanes), jnp.float32)
    return pl.pallas_call(
        functools.partial(fused, ctx, chans),
        out_shape=pltpu.VMEM((width, tokens), jnp.bfloat16),
        in_specs=[pl.BlockSpec(memory_space=pltpu.HBM)] * 6,
        out_specs=vmem,
        scratch_shapes=[
            pltpu.VMEM(proj.shape, proj.dtype),
            pltpu.VMEM(taps.shape, taps.dtype),
            pltpu.VMEM((modes, width), jnp.float32),
            pltpu.VMEM((modes, width), jnp.float32),
            pltpu.VMEM((1, width), jnp.float32),
            pltpu.VMEM((3, width, BLOCK), jnp.bfloat16),
            major,
            major,
            major,
            pltpu.VMEM((3, groups, BLOCK, 2 * BLOCK), jnp.bfloat16),
            table,
            table,
            table,
            pltpu.VMEM((ctx - 1, modes * groups, lanes), jnp.float32),
            weight_scratch,
            gath_scratch,
            pltpu.SemaphoreType.DMA,
            pltpu.SemaphoreType.DMA((5,)),
            pltpu.SemaphoreType.DMA((2,)),
            pltpu.SemaphoreType.DMA((ctx - 1,)),
            pltpu.SemaphoreType.DMA((ctx - 1,)),
            *rest,
        ],
        compiler_params=pltpu.CompilerParams(
            vmem_limit_bytes=58 << 20, collective_id=0, has_side_effects=True
        ),
        name="fused",
    )(proj, taps, rate.T, residue.T, skip.reshape(1, width), out_weight)


def solution(mesh):
    in_specs = (P(None, "chan", "ctx"), P(), P("chan", None), P("chan", None), P("chan"), P())
    out_specs = P("chan", "ctx")
    return jax.shard_map(
        functools.partial(per_device, mesh.shape["ctx"], mesh.shape["chan"]),
        mesh=mesh,
        in_specs=in_specs,
        out_specs=out_specs,
        check_vma=False,
    )
```

```python
import functools
import jax
import jax.numpy as jnp
from jax import lax
from jax.experimental import pallas as pl
from jax.experimental.pallas import tpu as pltpu
from jax.sharding import PartitionSpec as P

GROUP = 16
BLOCK = 128
PIECES = 4
MESH = pl.DeviceIdType.MESH
HIGHEST = lax.Precision.HIGHEST


def iota(shape, axis):
    return lax.broadcasted_iota(jnp.int32, shape, axis)


def one_hot(hit, dtype=jnp.float32):
    return hit.astype(jnp.float32).astype(dtype)


def ring_place(chan, n):
    row, side = chan // 2, chan % 2
    return row + side * (n - 1 - 2 * row)


def ring_chan(place, n):
    side = place // (n // 2)
    row = place + side * (n - 1 - 2 * place)
    return 2 * row + side


def turned_tiles(work, groups, blocks, put):
    for g in range(groups):
        turned = work[pl.ds(g, BLOCK, stride=groups), :].astype(jnp.bfloat16).T
        for b in range(blocks):
            put(g, b, turned[b * GROUP : (b + 1) * GROUP])


def exchange(
    chans,
    chan,
    work,
    gath,
    weight,
    weight_copy,
    out_ref,
    parts,
    turned_weight,
    results,
    there_send,
    there_recv,
    back_send,
    back_recv,
):
    width = out_ref.shape[0]
    groups = width // GROUP

    def put(g, b, tile):
        parts[b, g * GROUP : (g + 1) * GROUP, :] = tile

    turned_tiles(work, groups, chans, put)
    order = sorted(range(1, chans), key=lambda hop: -min(hop, chans - hop))
    there, back = {}, {}
    for hop in order:
        peer = (chan + hop) % chans
        there[hop] = pltpu.make_async_remote_copy(
            src_ref=parts.at[peer],
            dst_ref=gath.at[chan],
            send_sem=there_send.at[hop - 1],
            recv_sem=there_recv.at[hop - 1],
            device_id={"chan": peer},
            device_id_type=MESH,
        )
        there[hop].start()
    gath[chan] = parts[chan]
    weight_copy.wait()
    turned_weight[...] = weight[...].T
    for hop in order:
        there[hop].wait_recv()
    everything = gath[...].reshape(chans * width, BLOCK)

    def project(shard):
        rows_of = pl.ds(pl.multiple_of(shard * width, width), width)
        return jnp.dot(
            turned_weight[rows_of, :], everything, preferred_element_type=jnp.float32
        ).astype(jnp.bfloat16)

    own_columns = pl.ds(pl.multiple_of(chan * BLOCK, BLOCK), BLOCK)
    for hop in order:
        peer = (chan + hop) % chans
        results[hop - 1] = project(peer)
        back[hop] = pltpu.make_async_remote_copy(
            src_ref=results.at[hop - 1],
            dst_ref=out_ref.at[:, own_columns],
            send_sem=back_send.at[hop - 1],
            recv_sem=back_recv.at[hop - 1],
            device_id={"chan": peer},
            device_id_type=MESH,
        )
        back[hop].start()
    out_ref[:, own_columns] = project(chan)
    for hop in order:
        back[hop].wait_recv()
    for hop in order:
        there[hop].wait_send()
        back[hop].wait_send()


def ring(
    chans,
    chan,
    place,
    left,
    right,
    work,
    gath,
    own_weight,
    weight_copy,
    out_ref,
    acc,
    ring_send,
    ring_recv,
):
    width, tokens = out_ref.shape
    groups, blocks = width // GROUP, tokens // BLOCK
    cols = tokens // PIECES
    per_piece = blocks // PIECES

    def put(g, b, tile):
        inside = (b % per_piece) * BLOCK
        gath[
            chan, b // per_piece, g * GROUP : (g + 1) * GROUP, inside : inside + BLOCK
        ] = tile

    turned_tiles(work, groups, blocks, put)
    half = chans // 2

    def ring_copy(way, hop, piece):
        shard = ring_chan((place + chans + (-hop if way == 0 else hop)) % chans, chans)
        return pltpu.make_async_remote_copy(
            src_ref=gath.at[shard, piece],
            dst_ref=gath.at[shard, piece],
            send_sem=ring_send.at[way, hop, piece],
            recv_sem=ring_recv.at[way, hop, piece],
            device_id={"chan": right if way == 0 else left},
            device_id_type=MESH,
        )

    def travels(way, hop, piece):
        if hop < half - 1:
            return True
        return hop == half - 1 and (piece < PIECES // 2) == (way == 0)

    copies = {}
    for piece in range(PIECES):
        for way in range(2):
            copies[way, 0, piece] = ring_copy(way, 0, piece)
            copies[way, 0, piece].start()
    weight_copy.wait()

    def project(shard, piece):
        rows_of = pl.ds(pl.multiple_of(shard * width, width), width)
        return lax.dot_general(
            own_weight[rows_of, :],
            gath[shard, piece],
            (((0,), (0,)), ((), ())),
            preferred_element_type=jnp.float32,
        )

    for piece in range(PIECES):
        acc[piece] = project(chan, piece)
    for hop in range(1, half + 1):
        for piece in range(PIECES):
            arrived = []
            for way in range(2):
                if not travels(way, hop - 1, piece):
                    continue
                copies[way, hop - 1, piece].wait_recv()
                if travels(way, hop, piece):
                    copies[way, hop, piece] = ring_copy(way, hop, piece)
                    copies[way, hop, piece].start()
                arrived.append(
                    ring_chan((place + chans + (-hop if way == 0 else hop)) % chans, chans)
                )
            total = acc[piece]
            for shard in arrived:
                total = total + project(shard, piece)
            if hop == half:
                out_ref[:, piece * cols : (piece + 1) * cols] = total.astype(out_ref.dtype)
            else:
                acc[piece] = total

    for key in copies:
        copies[key].wait_send()


def flipped(chan, bit):
    return chan + bit * (1 - 2 * (chan // bit % 2))


def greet(chan, bit, sem):
    pl.semaphore_signal(
        sem, inc=1, device_id={"chan": flipped(chan, bit)}, device_id_type=MESH
    )


def met(sem):
    pl.semaphore_wait(sem, 1)


def is_swap(chans, width, tokens):
    return chans == 8 and width == BLOCK and tokens == chans * BLOCK


def fused(
    ctx,
    chans,
    proj_in,
    taps_in,
    rate_in,
    residue_in,
    skip_in,
    weight_ref,
    out_ref,
    proj_ref,
    taps_ref,
    rate_ref,
    residue_ref,
    skip_ref,
    halo,
    query,
    mixed,
    work,
    bands,
    rate_s,
    residue_s,
    state,
    own_end,
    ends,
    own_weight,
    gath,
    weight_sem,
    load_sems,
    halo_sems,
    end_send,
    end_recv,
    meet_sems,
    *rest,
):
    width, tokens = proj_ref.shape[1:]
    modes = rate_ref.shape[0]
    groups, blocks = width // GROUP, tokens // BLOCK
    lanes = blocks * GROUP
    planes = -(-modes // blocks)
    swap = is_swap(chans, width, tokens)
    index = lax.axis_index("ctx")
    chan = lax.axis_index("chan")
    bits = [1 << k for k in range(chans.bit_length() - 1)]
    if swap:
        peers = [flipped(chan, bit) for bit in bits]
    else:
        place = ring_place(chan, chans)
        right = ring_chan((place + 1) % chans, chans)
        left = ring_chan((place + chans - 1) % chans, chans)
        peers = [left, right]

    barrier = pltpu.get_barrier_semaphore()
    for hop in range(1, ctx):
        pl.semaphore_signal(
            barrier, inc=1, device_id={"ctx": (index + hop) % ctx}, device_id_type=MESH
        )
    for peer in peers:
        pl.semaphore_signal(barrier, inc=1, device_id={"chan": peer}, device_id_type=MESH)

    loads = [
        pltpu.make_async_copy(source, target, load_sems.at[k])
        for k, (source, target) in enumerate(
            (
                (taps_in, taps_ref),
                (rate_in, rate_ref),
                (residue_in, residue_ref),
                (skip_in, skip_ref),
                (proj_in, proj_ref),
            )
        )
    ]
    for load in loads:
        load.start()
    if swap or weight_ref.shape[1] == width:
        weight_from = weight_ref
    else:
        weight_from = weight_ref.at[:, pl.ds(pl.multiple_of(chan * width, width), width)]
    weight_copy = pltpu.make_async_copy(weight_from, own_weight, weight_sem)
    weight_copy.start()

    pl.semaphore_wait(barrier, ctx - 1 + len(peers))
    halo_copies = [
        pltpu.make_async_remote_copy(
            src_ref=proj_in.at[streams, :, pl.ds(tokens - BLOCK, BLOCK)],
            dst_ref=halo.at[streams],
            send_sem=halo_sems.at[2 * k],
            recv_sem=halo_sems.at[2 * k + 1],
            device_id={"ctx": (index + 1) % ctx},
            device_id_type=MESH,
        )
        for k, streams in enumerate((pl.ds(1, 2), pl.ds(0, 1)))
    ]

    @pl.when(index < ctx - 1)
    def _():
        for copy in halo_copies:
            copy.start()

    if swap:
        greet(chan, bits[1], meet_sems.at[0])

    loads[0].wait()
    all_groups = taps_ref.shape[1]
    pick = one_hot(
        iota((groups, all_groups), 1) == iota((groups, all_groups), 0) + chan * groups,
        jnp.bfloat16,
    )
    flip = one_hot(
        iota((BLOCK, 2 * BLOCK), 1) == BLOCK - iota((BLOCK, 2 * BLOCK), 0), jnp.bfloat16
    )
    def make_bands(stream):
        own = jnp.dot(pick, taps_ref[stream], preferred_element_type=jnp.float32)
        rows = jnp.dot(own.astype(jnp.bfloat16), flip, preferred_element_type=jnp.float32)
        for g in range(groups):
            wide = jnp.broadcast_to(rows[g : g + 1, :], (BLOCK, 2 * BLOCK))
            bands[stream, g] = pltpu.roll(wide, 0, 1, stride=1, stride_axis=0).astype(
                jnp.bfloat16
            )

    make_bands(1)
    make_bands(2)
    loads[1].wait()
    high = modes * groups
    expand = one_hot(iota((high, modes), 0) // groups == iota((high, modes), 1))
    kept = iota((high, width), 1) // GROUP == iota((high, width), 0) % groups
    spread = one_hot(iota((width, lanes), 0) % GROUP == iota((width, lanes), 1) % GROUP)

    def spread_rows(value):
        tall = lax.dot_general(
            expand,
            value,
            (((1,), (0,)), ((), ())),
            precision=HIGHEST,
            preferred_element_type=jnp.float32,
        )
        return jnp.dot(
            jnp.where(kept, tall, 0.0),
            spread,
            precision=HIGHEST,
            preferred_element_type=jnp.float32,
        )

    rate_s[...] = spread_rows(rate_ref[...])

    def of_mode(ref, m):
        return ref[m * groups : (m + 1) * groups, :]

    decay = [jnp.exp(-of_mode(rate_s, m)) for m in range(modes)]

    loads[4].wait()

    @pl.when(index > 0)
    def _():
        halo_copies[0].wait_recv()

    @pl.when(index == 0)
    def _():
        halo[...] = jnp.zeros_like(halo)

    def short(stream, g):
        rows_of = slice(g * GROUP, (g + 1) * GROUP)
        tiles = [proj_ref[stream, rows_of, b * BLOCK : (b + 1) * BLOCK] for b in range(blocks)]
        before = [halo[stream, rows_of, :]] + tiles[:-1]
        signal = jnp.concatenate(
            [jnp.concatenate(before, axis=0), jnp.concatenate(tiles, axis=0)], axis=1
        )
        return lax.dot_general(
            bands[stream, g], signal, (((1,), (1,)), ((), ())), preferred_element_type=jnp.float32
        )

    for g in range(groups):
        mixed[pl.ds(g, BLOCK, stride=groups), :] = short(1, g) * short(2, g)

    def gather_step(r, states):
        x = mixed[pl.ds(pl.multiple_of(r * groups, groups), groups), :]
        return tuple(d * s + x for d, s in zip(decay, states))

    zero = jnp.zeros((groups, lanes), jnp.float32)
    last = lax.fori_loop(0, BLOCK, gather_step, (zero,) * modes, unroll=16)
    at = iota(zero.shape, 1) // GROUP
    for m in range(modes):
        total, hop = last[m], 1
        while hop < blocks:
            moved = jnp.exp(of_mode(rate_s, m) * (-float(BLOCK * hop))) * pltpu.roll(
                total, GROUP * hop, 1
            )
            total = total + jnp.where(at >= hop, moved, 0.0)
            hop *= 2
        state[m * groups : (m + 1) * groups, :] = total
        plane, slot = m // blocks, m % blocks
        placed = jnp.where(at == slot, pltpu.roll(total, GROUP * ((slot + 1) % blocks), 1), 0.0)
        packed = placed if slot == 0 else packed + placed
        if slot == blocks - 1 or m == modes - 1:
            own_end[plane * groups : (plane + 1) * groups, :] = packed

    end_copies = [
        pltpu.make_async_remote_copy(
            src_ref=own_end,
            dst_ref=ends.at[hop - 1],
            send_sem=end_send.at[hop - 1],
            recv_sem=end_recv.at[hop - 1],
            device_id={"ctx": (index + hop) % ctx},
            device_id_type=MESH,
        )
        for hop in range(1, ctx)
    ]
    for hop in range(1, ctx):

        @pl.when(index < ctx - hop)
        def _():
            end_copies[hop - 1].start()

    if swap:
        met(meet_sems.at[0])
        greet(chan, bits[0], meet_sems.at[1])
    make_bands(0)

    @pl.when(index > 0)
    def _():
        halo_copies[1].wait_recv()

    for g in range(groups):
        query[pl.ds(g, BLOCK, stride=groups), :] = short(0, g)
    loads[2].wait()
    loads[3].wait()
    residue_s[...] = spread_rows(residue_ref[...]) * jnp.sqrt(2.0 * rate_s[...] / modes)
    skip_rows = jnp.where(
        iota((groups, width), 1) // GROUP == iota((groups, width), 0),
        jnp.broadcast_to(skip_ref[...], (groups, width)),
        0.0,
    )
    skip = jnp.dot(skip_rows, spread, precision=HIGHEST, preferred_element_type=jnp.float32)
    at_tokens = at.astype(jnp.float32) * float(BLOCK)
    planes = -(-modes // blocks)
    across = []
    for plane in range(planes):
        rates = of_mode(rate_s, plane * blocks)
        for m in range(plane * blocks + 1, min(modes, (plane + 1) * blocks)):
            rates = jnp.where(at == m % blocks, of_mode(rate_s, m), rates)
        across.append(jnp.exp(rates * (-float(tokens))))
    shift = [jnp.exp(-of_mode(rate_s, m) * at_tokens) for m in range(modes)]

    for hop in range(1, ctx):

        @pl.when(index >= hop)
        def _():
            end_copies[hop - 1].wait_recv()

        @pl.when(index < hop)
        def _():
            ends[hop - 1] = jnp.zeros((planes * groups, lanes), jnp.float32)

    arrived = []
    for plane in range(planes):
        total = jnp.zeros_like(zero)
        for hop in range(ctx - 1, 0, -1):
            total = across[plane] * total + ends[hop - 1, plane * groups : (plane + 1) * groups, :]
        arrived.append(total)
    entry, weight = [], []
    for m in range(modes):
        incoming = jnp.where(at == m % blocks, arrived[m // blocks], 0.0)
        hop = 1
        while hop < blocks:
            incoming = incoming + pltpu.roll(incoming, GROUP * hop, 1)
            hop *= 2
        own = jnp.where(at >= 1, pltpu.roll(of_mode(state, m), GROUP, 1), 0.0)
        entry.append(own + shift[m] * incoming)
        weight.append(of_mode(residue_s, m))

    def step(r, states):
        where = pl.ds(pl.multiple_of(r * groups, groups), groups)
        x = mixed[where, :]
        new = tuple(d * s + x for d, s in zip(decay, states))
        parts = [w * s for w, s in zip(weight, new)] + [skip * x]
        while len(parts) > 1:
            parts = [a + b for a, b in zip(parts[::2], parts[1::2])] + (
                [parts[-1]] if len(parts) % 2 else []
            )
        work[where, :] = query[where, :] * parts[0]
        return new

    lax.fori_loop(0, BLOCK, step, tuple(entry), unroll=8)
    if swap:
        met(meet_sems.at[1])
        exchange(chans, chan, work, gath, own_weight, weight_copy, out_ref, *rest)
    else:
        ring(chans, chan, place, left, right, work, gath, own_weight, weight_copy, out_ref, *rest)

    @pl.when(index < ctx - 1)
    def _():
        for copy in halo_copies:
            copy.wait_send()

    for hop in range(1, ctx):

        @pl.when(index < ctx - hop)
        def _():
            end_copies[hop - 1].wait_send()


def per_device(ctx, chans, proj, taps, rate, residue, skip, out_weight):
    width, tokens = proj.shape[1:]
    modes = rate.shape[1]
    groups, blocks = width // GROUP, tokens // BLOCK
    lanes = blocks * GROUP
    planes = -(-modes // blocks)
    swap = is_swap(chans, width, tokens)
    if width % 128:
        out_weight = lax.dynamic_slice_in_dim(
            out_weight, lax.axis_index("chan") * width, width, 1
        )
    vmem = pl.BlockSpec(memory_space=pltpu.VMEM)
    if swap:
        blocks_of = pltpu.VMEM((chans, width, BLOCK), jnp.bfloat16)
        square = pltpu.VMEM(out_weight.shape, jnp.bfloat16)
        several = pltpu.SemaphoreType.DMA((chans - 1,))
        weight_scratch, gath_scratch = square, blocks_of
        rest = [blocks_of, square, blocks_of] + [several] * 4
    else:
        weight_scratch = pltpu.VMEM((chans * width, width), jnp.bfloat16)
        gath_scratch = pltpu.VMEM((chans, PIECES, width, tokens // PIECES), jnp.bfloat16)
        hops = pltpu.SemaphoreType.DMA((2, chans // 2, PIECES))
        rest = [pltpu.VMEM((PIECES, width, tokens // PIECES), jnp.float32), hops, hops]
    major = pltpu.VMEM((BLOCK * groups, lanes), jnp.float32)
    table = pltpu.VMEM((modes * groups, lanes), jnp.float32)
    return pl.pallas_call(
        functools.partial(fused, ctx, chans),
        out_shape=pltpu.VMEM((width, tokens), jnp.bfloat16),
        in_specs=[pl.BlockSpec(memory_space=pltpu.HBM)] * 6,
        out_specs=vmem,
        scratch_shapes=[
            pltpu.VMEM(proj.shape, proj.dtype),
            pltpu.VMEM(taps.shape, taps.dtype),
            pltpu.VMEM((modes, width), jnp.float32),
            pltpu.VMEM((modes, width), jnp.float32),
            pltpu.VMEM((1, width), jnp.float32),
            pltpu.VMEM((3, width, BLOCK), jnp.bfloat16),
            major,
            major,
            major,
            pltpu.VMEM((3, groups, BLOCK, 2 * BLOCK), jnp.bfloat16),
            table,
            table,
            table,
            pltpu.VMEM((planes * groups, lanes), jnp.float32),
            pltpu.VMEM((ctx - 1, planes * groups, lanes), jnp.float32),
            weight_scratch,
            gath_scratch,
            pltpu.SemaphoreType.DMA,
            pltpu.SemaphoreType.DMA((5,)),
            pltpu.SemaphoreType.DMA((4,)),
            pltpu.SemaphoreType.DMA((ctx - 1,)),
            pltpu.SemaphoreType.DMA((ctx - 1,)),
            pltpu.SemaphoreType.REGULAR((2,)),
            *rest,
        ],
        compiler_params=pltpu.CompilerParams(
            vmem_limit_bytes=58 << 20, collective_id=0, has_side_effects=True
        ),
        name="fused",
    )(proj, taps, rate.T, residue.T, skip.reshape(1, width), out_weight)


def solution(mesh):
    in_specs = (P(None, "chan", "ctx"), P(), P("chan", None), P("chan", None), P("chan"), P())
    out_specs = P("chan", "ctx")
    return jax.shard_map(
        functools.partial(per_device, mesh.shape["ctx"], mesh.shape["chan"]),
        mesh=mesh,
        in_specs=in_specs,
        out_specs=out_specs,
        check_vma=False,
    )
```

```python
import functools
import jax
import jax.numpy as jnp
from jax import lax
from jax.experimental import pallas as pl
from jax.experimental.pallas import tpu as pltpu
from jax.sharding import PartitionSpec as P

GROUP = 16
BLOCK = 128
PIECES = 4
MESH = pl.DeviceIdType.MESH
HIGHEST = lax.Precision.HIGHEST


def iota(shape, axis):
    return lax.broadcasted_iota(jnp.int32, shape, axis)


def one_hot(hit, dtype=jnp.float32):
    return hit.astype(jnp.float32).astype(dtype)


def ring_place(chan, n):
    row, side = chan // 2, chan % 2
    return row + side * (n - 1 - 2 * row)


def ring_chan(place, n):
    side = place // (n // 2)
    row = place + side * (n - 1 - 2 * place)
    return 2 * row + side


def exchange(
    chans,
    chan,
    gath,
    weight,
    weight_copy,
    out_ref,
    parts,
    turned_weight,
    results,
    there,
    back_send,
    back_recv,
):
    width = out_ref.shape[0]
    gath[chan] = parts[chan]
    weight_copy.wait()
    turned_weight[...] = weight[...].T
    for copy in there:
        copy.wait_recv()
    everything = gath[...].reshape(chans * width, BLOCK)

    def project(shard):
        rows_of = pl.ds(pl.multiple_of(shard * width, width), width)
        return jnp.dot(
            turned_weight[rows_of, :], everything, preferred_element_type=jnp.float32
        ).astype(jnp.bfloat16)

    own_columns = pl.ds(pl.multiple_of(chan * BLOCK, BLOCK), BLOCK)
    back = []
    for mask in range(chans - 1, 0, -1):
        peer = flipped(chan, mask)
        results[mask - 1] = project(peer)
        back.append(
            pltpu.make_async_remote_copy(
                src_ref=results.at[mask - 1],
                dst_ref=out_ref.at[:, own_columns],
                send_sem=back_send.at[mask - 1],
                recv_sem=back_recv.at[mask - 1],
                device_id={"chan": peer},
                device_id_type=MESH,
            )
        )
        back[-1].start()
    out_ref[:, own_columns] = project(chan)
    for copy in back:
        copy.wait_recv()
    for copy in there + back:
        copy.wait_send()


def ring(
    chans,
    chan,
    place,
    left,
    right,
    gath,
    own_weight,
    weight_copy,
    out_ref,
    acc,
    ring_send,
    ring_recv,
):
    width, tokens = out_ref.shape
    cols = tokens // PIECES
    half = chans // 2

    def ring_copy(way, hop, piece):
        shard = ring_chan((place + chans + (-hop if way == 0 else hop)) % chans, chans)
        return pltpu.make_async_remote_copy(
            src_ref=gath.at[shard, piece],
            dst_ref=gath.at[shard, piece],
            send_sem=ring_send.at[way, hop, piece],
            recv_sem=ring_recv.at[way, hop, piece],
            device_id={"chan": right if way == 0 else left},
            device_id_type=MESH,
        )

    def travels(way, hop, piece):
        if hop < half - 1:
            return True
        return hop == half - 1 and (piece < PIECES // 2) == (way == 0)

    copies = {}
    for piece in range(PIECES):
        for way in range(2):
            copies[way, 0, piece] = ring_copy(way, 0, piece)
            copies[way, 0, piece].start()
    weight_copy.wait()

    def project(shard, piece):
        rows_of = pl.ds(pl.multiple_of(shard * width, width), width)
        return lax.dot_general(
            own_weight[rows_of, :],
            gath[shard, piece],
            (((0,), (0,)), ((), ())),
            preferred_element_type=jnp.float32,
        )

    for piece in range(PIECES):
        acc[piece] = project(chan, piece)
    for hop in range(1, half + 1):
        for piece in range(PIECES):
            arrived = []
            for way in range(2):
                if not travels(way, hop - 1, piece):
                    continue
                copies[way, hop - 1, piece].wait_recv()
                if travels(way, hop, piece):
                    copies[way, hop, piece] = ring_copy(way, hop, piece)
                    copies[way, hop, piece].start()
                arrived.append(
                    ring_chan((place + chans + (-hop if way == 0 else hop)) % chans, chans)
                )
            total = acc[piece]
            for shard in arrived:
                total = total + project(shard, piece)
            if hop == half:
                out_ref[:, piece * cols : (piece + 1) * cols] = total.astype(out_ref.dtype)
            else:
                acc[piece] = total

    for key in copies:
        copies[key].wait_send()


def flipped(chan, mask):
    peer, bit = chan, 1
    while bit <= mask:
        if mask & bit:
            peer = peer + bit * (1 - 2 * (chan // bit % 2))
        bit *= 2
    return peer


def greet(chan, bit, sem):
    pl.semaphore_signal(
        sem, inc=1, device_id={"chan": flipped(chan, bit)}, device_id_type=MESH
    )


def met(sem):
    pl.semaphore_wait(sem, 1)


def is_swap(chans, width, tokens):
    return chans == 8 and width == BLOCK and tokens == chans * BLOCK


def split_of(groups):
    return 2 if groups % 2 == 0 else 1


def doubling(end):
    hops = [1]
    while hops[-1] * 2 < end:
        hops.append(hops[-1] * 2)
    return hops if end > 1 else []


def fused(
    ctx,
    chans,
    proj_in,
    taps_in,
    rate_in,
    residue_in,
    skip_in,
    weight_ref,
    out_ref,
    proj_ref,
    taps_ref,
    rate_ref,
    residue_ref,
    skip_ref,
    halo,
    query,
    mixed,
    work,
    bands,
    tall,
    rate_s,
    residue_s,
    powers,
    across,
    inner,
    outer,
    own_end,
    ends,
    own_weight,
    gath,
    weight_sem,
    load_sems,
    halo_sems,
    end_send,
    end_recv,
    meet_sems,
    *rest,
):
    width, tokens = proj_ref.shape[1:]
    modes = rate_ref.shape[0]
    groups, blocks = width // GROUP, tokens // BLOCK
    lanes = blocks * GROUP
    split = split_of(groups)
    per, span, half = groups // split, BLOCK // split, width // split
    planes = own_end.shape[1] // groups
    swap = is_swap(chans, width, tokens)
    index = lax.axis_index("ctx")
    chan = lax.axis_index("chan")
    bits = [1 << k for k in range(chans.bit_length() - 1)]
    if swap:
        peers = [flipped(chan, bit) for bit in bits]
        parts, turned_weight, results, there_send, there_recv, back_send, back_recv = rest
    else:
        place = ring_place(chan, chans)
        right = ring_chan((place + 1) % chans, chans)
        left = ring_chan((place + chans - 1) % chans, chans)
        peers = [left, right]

    barrier = pltpu.get_barrier_semaphore()
    for hop in range(1, ctx):
        pl.semaphore_signal(
            barrier, inc=1, device_id={"ctx": (index + hop) % ctx}, device_id_type=MESH
        )
    for peer in peers:
        pl.semaphore_signal(barrier, inc=1, device_id={"chan": peer}, device_id_type=MESH)

    loads = [
        pltpu.make_async_copy(source, target, load_sems.at[k])
        for k, (source, target) in enumerate(
            (
                (taps_in, taps_ref),
                (rate_in, rate_ref),
                (residue_in, residue_ref),
                (skip_in, skip_ref),
                (proj_in, proj_ref),
            )
        )
    ]
    for load in loads:
        load.start()
    if swap or weight_ref.shape[1] == width:
        weight_from = weight_ref
    else:
        weight_from = weight_ref.at[:, pl.ds(pl.multiple_of(chan * width, width), width)]
    weight_copy = pltpu.make_async_copy(weight_from, own_weight, weight_sem)
    weight_copy.start()

    loads[0].wait()
    all_groups = taps_ref.shape[1]
    pick = one_hot(
        iota((groups, all_groups), 1) == iota((groups, all_groups), 0) + chan * groups,
        jnp.bfloat16,
    )
    flip = one_hot(
        iota((BLOCK, 2 * BLOCK), 1) == BLOCK - iota((BLOCK, 2 * BLOCK), 0), jnp.bfloat16
    )

    def make_bands(stream):
        own = jnp.dot(pick, taps_ref[stream], preferred_element_type=jnp.float32)
        rows = jnp.dot(own.astype(jnp.bfloat16), flip, preferred_element_type=jnp.float32)
        for g in range(groups):
            wide = jnp.broadcast_to(rows[g : g + 1, :], (BLOCK, 2 * BLOCK))
            bands[stream, g] = pltpu.roll(wide, 0, 1, stride=1, stride_axis=0).astype(
                jnp.bfloat16
            )

    make_bands(1)
    make_bands(2)

    pl.semaphore_wait(barrier, ctx - 1 + len(peers))
    halo_parts = [(pl.ds(1, 2), pl.ds(p * half, half)) for p in range(split)]
    halo_parts.append((pl.ds(0, 1), pl.ds(0, width)))
    halo_copies = [
        pltpu.make_async_remote_copy(
            src_ref=proj_in.at[streams, rows, pl.ds(tokens - BLOCK, BLOCK)],
            dst_ref=halo.at[streams, rows],
            send_sem=halo_sems.at[2 * k],
            recv_sem=halo_sems.at[2 * k + 1],
            device_id={"ctx": (index + 1) % ctx},
            device_id_type=MESH,
        )
        for k, (streams, rows) in enumerate(halo_parts)
    ]

    @pl.when(index < ctx - 1)
    def _():
        for copy in halo_copies:
            copy.start()

    @pl.when(index == 0)
    def _():
        halo[...] = jnp.zeros_like(halo)

    if swap:
        greet(chan, bits[1], meet_sems.at[0])

    shape = (groups, lanes)
    tile_at = iota(shape, 1) // GROUP
    part_at = iota(shape, 0) // per
    part_hops, tile_hops = doubling(split), doubling(blocks)
    spread = one_hot(iota((width, lanes), 0) % GROUP == iota((width, lanes), 1) % GROUP)

    def entry_rows(p, m, count=modes):
        return pl.ds((p * count + m) * groups, groups)

    def spread_rows(rows):
        count = len(rows)
        for p in range(split):
            kept = iota((groups, width), 1) // GROUP == p * per + iota((groups, width), 0) % per
            for m, row in enumerate(rows):
                tall[entry_rows(p, m, count), :] = jnp.where(
                    kept, jnp.broadcast_to(row, (groups, width)), 0.0
                )
        return jnp.dot(
            tall[0 : split * count * groups, :],
            spread,
            precision=HIGHEST,
            preferred_element_type=jnp.float32,
        )

    loads[1].wait()
    rate_s[...] = spread_rows([rate_ref[m : m + 1, :] for m in range(modes)])
    since = (part_at * span).astype(jnp.float32)
    kinds = (
        [1.0]
        + [float(span * hop) for hop in part_hops]
        + [float(BLOCK * hop) for hop in tile_hops]
        + [since, since + (tile_at * BLOCK).astype(jnp.float32)]
    )
    at_parts, at_tiles = 1, 1 + len(part_hops)
    at_since, at_shift = len(kinds) - 2, len(kinds) - 1

    def slot_of(m):
        return m // (blocks * split), m // blocks % split, m % blocks

    def in_slot(m):
        plane, part, tile = slot_of(m)
        return jnp.logical_and(part_at == part, tile_at == tile)

    for p in range(split):
        packed = [None] * planes
        for m in range(modes):
            rates = rate_s[entry_rows(p, m), :]
            for k, far in enumerate(kinds):
                powers[k, entry_rows(p, m), :] = jnp.exp(-rates * far)
            plane = slot_of(m)[0]
            packed[plane] = (
                rates if packed[plane] is None else jnp.where(in_slot(m), rates, packed[plane])
            )
        for plane in range(planes):
            across[p, plane * groups : (plane + 1) * groups, :] = jnp.exp(
                packed[plane] * (-float(tokens))
            )

    make_bands(0)
    loads[2].wait()
    loads[3].wait()
    skip_at = split * modes * groups
    wide_rates = rate_s[...]
    weights = spread_rows([residue_ref[m : m + 1, :] for m in range(modes)])
    residue_s[0:skip_at, :] = weights * jnp.sqrt(2.0 * wide_rates / modes)
    residue_s[skip_at : skip_at + split * groups, :] = spread_rows([skip_ref[...]])

    loads[4].wait()

    def short(stream, g):
        rows_of = slice(g * GROUP, (g + 1) * GROUP)
        tiles = [proj_ref[stream, rows_of, b * BLOCK : (b + 1) * BLOCK] for b in range(blocks)]
        before = [halo[stream, rows_of, :]] + tiles[:-1]
        signal = jnp.concatenate(
            [jnp.concatenate(before, axis=0), jnp.concatenate(tiles, axis=0)], axis=1
        )
        return lax.dot_general(
            bands[stream, g], signal, (((1,), (1,)), ((), ())), preferred_element_type=jnp.float32
        )

    def strided(p, part, inside):
        return pl.ds(p * span * groups + part * per + inside, span, stride=groups)

    def keep(ref, g, value):
        p, inside = g // per, g % per
        for part in range(split):
            ref[strided(p, part, inside), :] = value[part * span : (part + 1) * span]

    def step_rows(p, r):
        return pl.ds(pl.multiple_of((p * span + r) * groups, groups), groups)

    def power(k, p, m):
        return powers[k, entry_rows(p, m), :]

    zero = jnp.zeros(shape, jnp.float32)

    def end_copy(hop, p):
        return pltpu.make_async_remote_copy(
            src_ref=own_end.at[p],
            dst_ref=ends.at[hop - 1, p],
            send_sem=end_send.at[hop - 1, p],
            recv_sem=end_recv.at[hop - 1, p],
            device_id={"ctx": (index + hop) % ctx},
            device_id_type=MESH,
        )

    end_copies = {(hop, p): end_copy(hop, p) for hop in range(1, ctx) for p in range(split)}

    def first_pass(p):
        @pl.when(index > 0)
        def _():
            halo_copies[p].wait_recv()

        for g in range(p * per, (p + 1) * per):
            keep(mixed, g, short(1, g) * short(2, g))
        decay = [power(0, p, m) for m in range(modes)]

        def gather_step(r, states):
            x = mixed[step_rows(p, r), :]
            return tuple(d * s + x for d, s in zip(decay, states))

        last = lax.fori_loop(0, span, gather_step, (zero,) * modes, unroll=16)
        packed = [zero] * planes
        for m in range(modes):
            total = last[m]
            for k, hop in enumerate(part_hops):
                moved = power(at_parts + k, p, m) * pltpu.roll(total, per * hop, 0)
                total = total + jnp.where(part_at >= hop, moved, 0.0)
            inner[entry_rows(p, m), :] = total
            if split > 1:
                total = jnp.where(part_at == split - 1, total, 0.0)
                for hop in part_hops:
                    total = total + pltpu.roll(total, per * hop, 0)
            for k, hop in enumerate(tile_hops):
                moved = power(at_tiles + k, p, m) * pltpu.roll(total, GROUP * hop, 1)
                total = total + jnp.where(tile_at >= hop, moved, 0.0)
            outer[entry_rows(p, m), :] = total
            plane, part, tile = slot_of(m)
            placed = pltpu.roll(total, GROUP * ((tile + 1) % blocks), 1)
            packed[plane] = jnp.where(in_slot(m), placed, packed[plane])
        for plane in range(planes):
            own_end[p, plane * groups : (plane + 1) * groups, :] = packed[plane]
        for hop in range(1, ctx):

            @pl.when(index < ctx - hop)
            def _():
                end_copies[hop, p].start()

    def second_pass(p):
        for g in range(p * per, (p + 1) * per):
            keep(query, g, short(0, g))
        base = []
        for m in range(modes):
            own = power(at_since, p, m) * jnp.where(
                tile_at >= 1, pltpu.roll(outer[entry_rows(p, m), :], GROUP, 1), 0.0
            )
            if split > 1:
                own = own + jnp.where(
                    part_at >= 1, pltpu.roll(inner[entry_rows(p, m), :], per, 0), 0.0
                )
            inner[entry_rows(p, m), :] = own
        for hop in range(1, ctx):

            @pl.when(index >= hop)
            def _():
                end_copies[hop, p].wait_recv()

            @pl.when(index < hop)
            def _():
                ends[hop - 1, p] = jnp.zeros(ends.shape[2:], jnp.float32)

        arrived = []
        for plane in range(planes):
            rows = slice(plane * groups, (plane + 1) * groups)
            total = zero
            for hop in range(ctx - 1, 0, -1):
                total = across[p, rows, :] * total + ends[hop - 1, p, rows, :]
            arrived.append(total)
        entry = []
        for m in range(modes):
            incoming = jnp.where(in_slot(m), arrived[slot_of(m)[0]], 0.0)
            for hop in part_hops:
                incoming = incoming + pltpu.roll(incoming, per * hop, 0)
            for hop in tile_hops:
                incoming = incoming + pltpu.roll(incoming, GROUP * hop, 1)
            entry.append(inner[entry_rows(p, m), :] + power(at_shift, p, m) * incoming)
        decay = [power(0, p, m) for m in range(modes)]
        weight = [residue_s[entry_rows(p, m), :] for m in range(modes)]
        skip = residue_s[pl.ds(skip_at + p * groups, groups), :]

        def step(r, states):
            where = step_rows(p, r)
            x = mixed[where, :]
            new = tuple(d * s + x for d, s in zip(decay, states))
            terms = [w * s for w, s in zip(weight, new)] + [skip * x]
            while len(terms) > 1:
                terms = [a + b for a, b in zip(terms[::2], terms[1::2])] + (
                    [terms[-1]] if len(terms) % 2 else []
                )
            work[where, :] = query[where, :] * terms[0]
            return new

        lax.fori_loop(0, span, step, tuple(entry), unroll=8)

    def turn(p, put):
        for inside in range(per):
            rows = [work[strided(p, part, inside), :] for part in range(split)]
            whole = jnp.concatenate(rows, axis=0) if split > 1 else rows[0]
            turned = whole.astype(jnp.bfloat16).T
            for b in range(blocks):
                put(p * per + inside, b, turned[b * GROUP : (b + 1) * GROUP])

    for p in range(split):
        first_pass(p)
    if swap:
        met(meet_sems.at[0])
        greet(chan, bits[0], meet_sems.at[1])

    @pl.when(index > 0)
    def _():
        halo_copies[split].wait_recv()

    if swap:
        there = []

        def put(g, b, tile):
            parts[b, g * GROUP : (g + 1) * GROUP, :] = tile

        for p in range(split):
            second_pass(p)
            turn(p, put)
            if p == 0:
                met(meet_sems.at[1])
            rows = pl.ds(p * half, half)
            for mask in range(chans - 1, 0, -1):
                peer = flipped(chan, mask)
                there.append(
                    pltpu.make_async_remote_copy(
                        src_ref=parts.at[peer, rows],
                        dst_ref=gath.at[chan, rows],
                        send_sem=there_send.at[p, mask - 1],
                        recv_sem=there_recv.at[p, mask - 1],
                        device_id={"chan": peer},
                        device_id_type=MESH,
                    )
                )
                there[-1].start()
        exchange(
            chans,
            chan,
            gath,
            own_weight,
            weight_copy,
            out_ref,
            parts,
            turned_weight,
            results,
            there,
            back_send,
            back_recv,
        )
    else:
        per_piece = blocks // PIECES

        def put(g, b, tile):
            inside = (b % per_piece) * BLOCK
            gath[
                chan, b // per_piece, g * GROUP : (g + 1) * GROUP, inside : inside + BLOCK
            ] = tile

        for p in range(split):
            second_pass(p)
            turn(p, put)
        ring(chans, chan, place, left, right, gath, own_weight, weight_copy, out_ref, *rest)

    @pl.when(index < ctx - 1)
    def _():
        for copy in halo_copies:
            copy.wait_send()

    for hop in range(1, ctx):

        @pl.when(index < ctx - hop)
        def _():
            for p in range(split):
                end_copies[hop, p].wait_send()


def per_device(ctx, chans, proj, taps, rate, residue, skip, out_weight):
    width, tokens = proj.shape[1:]
    modes = rate.shape[1]
    groups, blocks = width // GROUP, tokens // BLOCK
    lanes = blocks * GROUP
    split = split_of(groups)
    planes = -(-modes // (blocks * split))
    kinds = 3 + len(doubling(split)) + len(doubling(blocks))
    swap = is_swap(chans, width, tokens)
    if width % 128:
        out_weight = lax.dynamic_slice_in_dim(
            out_weight, lax.axis_index("chan") * width, width, 1
        )
    vmem = pl.BlockSpec(memory_space=pltpu.VMEM)
    if swap:
        blocks_of = pltpu.VMEM((chans, width, BLOCK), jnp.bfloat16)
        square = pltpu.VMEM(out_weight.shape, jnp.bfloat16)
        several = pltpu.SemaphoreType.DMA((chans - 1,))
        by_part = pltpu.SemaphoreType.DMA((split, chans - 1))
        weight_scratch, gath_scratch = square, blocks_of
        rest = [blocks_of, square, blocks_of, by_part, by_part, several, several]
    else:
        weight_scratch = pltpu.VMEM((chans * width, width), jnp.bfloat16)
        gath_scratch = pltpu.VMEM((chans, PIECES, width, tokens // PIECES), jnp.bfloat16)
        hops = pltpu.SemaphoreType.DMA((2, chans // 2, PIECES))
        rest = [pltpu.VMEM((PIECES, width, tokens // PIECES), jnp.float32), hops, hops]
    major = pltpu.VMEM((BLOCK * groups, lanes), jnp.float32)
    rows = split * modes * groups
    table = pltpu.VMEM((rows, lanes), jnp.float32)
    packed = (split, planes * groups, lanes)
    return pl.pallas_call(
        functools.partial(fused, ctx, chans),
        out_shape=pltpu.VMEM((width, tokens), jnp.bfloat16),
        in_specs=[pl.BlockSpec(memory_space=pltpu.HBM)] * 6,
        out_specs=vmem,
        scratch_shapes=[
            pltpu.VMEM(proj.shape, proj.dtype),
            pltpu.VMEM(taps.shape, taps.dtype),
            pltpu.VMEM((modes, width), jnp.float32),
            pltpu.VMEM((modes, width), jnp.float32),
            pltpu.VMEM((1, width), jnp.float32),
            pltpu.VMEM((3, width, BLOCK), jnp.bfloat16),
            major,
            major,
            major,
            pltpu.VMEM((3, groups, BLOCK, 2 * BLOCK), jnp.bfloat16),
            pltpu.VMEM((rows, width), jnp.float32),
            table,
            pltpu.VMEM((rows + split * groups, lanes), jnp.float32),
            pltpu.VMEM((kinds, rows, lanes), jnp.float32),
            pltpu.VMEM(packed, jnp.float32),
            table,
            table,
            pltpu.VMEM(packed, jnp.float32),
            pltpu.VMEM((ctx - 1, *packed), jnp.float32),
            weight_scratch,
            gath_scratch,
            pltpu.SemaphoreType.DMA,
            pltpu.SemaphoreType.DMA((5,)),
            pltpu.SemaphoreType.DMA((2 * (split + 1),)),
            pltpu.SemaphoreType.DMA((ctx - 1, split)),
            pltpu.SemaphoreType.DMA((ctx - 1, split)),
            pltpu.SemaphoreType.REGULAR((2,)),
            *rest,
        ],
        compiler_params=pltpu.CompilerParams(
            vmem_limit_bytes=58 << 20, collective_id=0, has_side_effects=True
        ),
        name="fused",
    )(proj, taps, rate.T, residue.T, skip.reshape(1, width), out_weight)


def solution(mesh):
    in_specs = (P(None, "chan", "ctx"), P(), P("chan", None), P("chan", None), P("chan"), P())
    out_specs = P("chan", "ctx")
    return jax.shard_map(
        functools.partial(per_device, mesh.shape["ctx"], mesh.shape["chan"]),
        mesh=mesh,
        in_specs=in_specs,
        out_specs=out_specs,
        check_vma=False,
    )
```

```python
import functools
import jax
import jax.numpy as jnp
from jax import lax
from jax.experimental import pallas as pl
from jax.experimental.pallas import tpu as pltpu
from jax.sharding import PartitionSpec as P

GROUP = 16
BLOCK = 128
PIECES = 4
SPLIT = 2
MESH = pl.DeviceIdType.MESH
HIGHEST = lax.Precision.HIGHEST


def iota(shape, axis):
    return lax.broadcasted_iota(jnp.int32, shape, axis)


def one_hot(hit, dtype=jnp.float32):
    return hit.astype(jnp.float32).astype(dtype)


def ring_place(chan, n):
    row, side = chan // 2, chan % 2
    return row + side * (n - 1 - 2 * row)


def ring_chan(place, n):
    side = place // (n // 2)
    row = place + side * (n - 1 - 2 * place)
    return 2 * row + side


def exchange(
    chans,
    chan,
    gath,
    weight,
    weight_copy,
    out_ref,
    parts,
    turned_weight,
    results,
    there,
    back_send,
    back_recv,
):
    width = out_ref.shape[0]
    gath[chan] = parts[chan]
    weight_copy.wait()
    turned_weight[...] = weight[...].T
    for copy in there:
        copy.wait_recv()
    everything = gath[...].reshape(chans * width, BLOCK)

    def project(shard):
        rows_of = pl.ds(pl.multiple_of(shard * width, width), width)
        return jnp.dot(
            turned_weight[rows_of, :], everything, preferred_element_type=jnp.float32
        ).astype(jnp.bfloat16)

    own_columns = pl.ds(pl.multiple_of(chan * BLOCK, BLOCK), BLOCK)
    back = []
    for mask in range(chans - 1, 0, -1):
        peer = flipped(chan, mask)
        results[mask - 1] = project(peer)
        back.append(
            pltpu.make_async_remote_copy(
                src_ref=results.at[mask - 1],
                dst_ref=out_ref.at[:, own_columns],
                send_sem=back_send.at[mask - 1],
                recv_sem=back_recv.at[mask - 1],
                device_id={"chan": peer},
                device_id_type=MESH,
            )
        )
        back[-1].start()
    out_ref[:, own_columns] = project(chan)
    for copy in back:
        copy.wait_recv()
    for copy in there + back:
        copy.wait_send()


def ring(
    chans,
    chan,
    place,
    left,
    right,
    gath,
    own_weight,
    weight_copy,
    out_ref,
    acc,
    ring_send,
    ring_recv,
):
    width, tokens = out_ref.shape
    cols = tokens // PIECES
    half = chans // 2

    def ring_copy(way, hop, piece):
        shard = ring_chan((place + chans + (-hop if way == 0 else hop)) % chans, chans)
        return pltpu.make_async_remote_copy(
            src_ref=gath.at[shard, piece],
            dst_ref=gath.at[shard, piece],
            send_sem=ring_send.at[way, hop, piece],
            recv_sem=ring_recv.at[way, hop, piece],
            device_id={"chan": right if way == 0 else left},
            device_id_type=MESH,
        )

    def travels(way, hop, piece):
        if hop < half - 1:
            return True
        return hop == half - 1 and (piece < PIECES // 2) == (way == 0)

    copies = {}
    for piece in range(PIECES):
        for way in range(2):
            copies[way, 0, piece] = ring_copy(way, 0, piece)
            copies[way, 0, piece].start()
    weight_copy.wait()

    def project(shard, piece):
        rows_of = pl.ds(pl.multiple_of(shard * width, width), width)
        return lax.dot_general(
            own_weight[rows_of, :],
            gath[shard, piece],
            (((0,), (0,)), ((), ())),
            preferred_element_type=jnp.float32,
        )

    for piece in range(PIECES):
        acc[piece] = project(chan, piece)
    for hop in range(1, half + 1):
        for piece in range(PIECES):
            arrived = []
            for way in range(2):
                if not travels(way, hop - 1, piece):
                    continue
                copies[way, hop - 1, piece].wait_recv()
                if travels(way, hop, piece):
                    copies[way, hop, piece] = ring_copy(way, hop, piece)
                    copies[way, hop, piece].start()
                arrived.append(
                    ring_chan((place + chans + (-hop if way == 0 else hop)) % chans, chans)
                )
            total = acc[piece]
            for shard in arrived:
                total = total + project(shard, piece)
            if hop == half:
                out_ref[:, piece * cols : (piece + 1) * cols] = total.astype(out_ref.dtype)
            else:
                acc[piece] = total

    for key in copies:
        copies[key].wait_send()


def flipped(chan, mask):
    peer, bit = chan, 1
    while bit <= mask:
        if mask & bit:
            peer = peer + bit * (1 - 2 * (chan // bit % 2))
        bit *= 2
    return peer


def greet(peer, sem):
    pl.semaphore_signal(sem, inc=1, device_id={"chan": peer}, device_id_type=MESH)


def is_swap(chans, width, tokens):
    return chans == 8 and width == BLOCK and tokens == chans * BLOCK


def split_of(groups):
    split = 1
    while split < SPLIT and groups % (2 * split) == 0:
        split *= 2
    return split


def doubling(end):
    hops = [1]
    while hops[-1] * 2 < end:
        hops.append(hops[-1] * 2)
    return hops if end > 1 else []


def fused(
    ctx,
    chans,
    proj_in,
    taps_in,
    rate_in,
    residue_in,
    skip_in,
    weight_ref,
    out_ref,
    proj_ref,
    taps_ref,
    rate_ref,
    residue_ref,
    skip_ref,
    halo,
    query,
    mixed,
    work,
    bands,
    tall,
    rate_s,
    residue_s,
    powers,
    across,
    inner,
    outer,
    own_end,
    ends,
    own_weight,
    gath,
    weight_sem,
    load_sems,
    halo_sems,
    end_send,
    end_recv,
    meet_sems,
    *rest,
):
    width, tokens = proj_ref.shape[1:]
    modes = rate_ref.shape[0]
    groups, blocks = width // GROUP, tokens // BLOCK
    lanes = blocks * GROUP
    split = split_of(groups)
    per, span, half = groups // split, BLOCK // split, width // split
    planes = own_end.shape[1] // groups
    swap = is_swap(chans, width, tokens)
    index = lax.axis_index("ctx")
    chan = lax.axis_index("chan")
    if swap:
        row, last_row = chan // 2, chans // 2 - 1
        peers = [(chan + 1 - 2 * (chan % 2), None), (chan - 2, row > 0), (chan + 2, row < last_row)]
        parts, turned_weight, results, there_send, there_recv, back_send, back_recv = rest
    else:
        place = ring_place(chan, chans)
        right = ring_chan((place + 1) % chans, chans)
        left = ring_chan((place + chans - 1) % chans, chans)
        peers = [(left, None), (right, None)]

    barrier = pltpu.get_barrier_semaphore()
    for hop in range(1, ctx):
        pl.semaphore_signal(
            barrier, inc=1, device_id={"ctx": (index + hop) % ctx}, device_id_type=MESH
        )
    expected = ctx - 1
    for peer, there_is in peers:
        if there_is is None:
            greet(peer, barrier)
            expected = expected + 1
        else:
            pl.when(there_is)(functools.partial(greet, peer, barrier))
            expected = expected + jnp.where(there_is, 1, 0)

    loads = [
        pltpu.make_async_copy(source, target, load_sems.at[k])
        for k, (source, target) in enumerate(
            (
                (taps_in, taps_ref),
                (rate_in, rate_ref),
                (residue_in, residue_ref),
                (skip_in, skip_ref),
                (proj_in, proj_ref),
            )
        )
    ]
    for load in loads:
        load.start()
    if swap or weight_ref.shape[1] == width:
        weight_from = weight_ref
    else:
        weight_from = weight_ref.at[:, pl.ds(pl.multiple_of(chan * width, width), width)]
    weight_copy = pltpu.make_async_copy(weight_from, own_weight, weight_sem)
    weight_copy.start()

    loads[0].wait()
    all_groups = taps_ref.shape[1]
    pick = one_hot(
        iota((groups, all_groups), 1) == iota((groups, all_groups), 0) + chan * groups,
        jnp.bfloat16,
    )
    flip = one_hot(
        iota((BLOCK, 2 * BLOCK), 1) == BLOCK - iota((BLOCK, 2 * BLOCK), 0), jnp.bfloat16
    )

    def make_bands(stream):
        own = jnp.dot(pick, taps_ref[stream], preferred_element_type=jnp.float32)
        rows = jnp.dot(own.astype(jnp.bfloat16), flip, preferred_element_type=jnp.float32)
        for g in range(groups):
            wide = jnp.broadcast_to(rows[g : g + 1, :], (BLOCK, 2 * BLOCK))
            bands[stream, g] = pltpu.roll(wide, 0, 1, stride=1, stride_axis=0).astype(
                jnp.bfloat16
            )

    make_bands(1)
    make_bands(2)

    loads[4].wait()
    pl.semaphore_wait(barrier, expected)
    halo_parts = [(pl.ds(1, 2), pl.ds(p * half, half)) for p in range(split)]
    halo_parts.append((pl.ds(0, 1), pl.ds(0, width)))
    halo_copies = [
        pltpu.make_async_remote_copy(
            src_ref=proj_ref.at[streams, rows, pl.ds(tokens - BLOCK, BLOCK)],
            dst_ref=halo.at[streams, rows],
            send_sem=halo_sems.at[2 * k],
            recv_sem=halo_sems.at[2 * k + 1],
            device_id={"ctx": (index + 1) % ctx},
            device_id_type=MESH,
        )
        for k, (streams, rows) in enumerate(halo_parts)
    ]

    @pl.when(index < ctx - 1)
    def _():
        for copy in halo_copies:
            copy.start()

    @pl.when(index == 0)
    def _():
        halo[...] = jnp.zeros_like(halo)

    if swap:
        up, down = meet_sems.at[0], meet_sems.at[1]

        @pl.when(row == 0)
        def _():
            greet(chan + 2, up)

        @pl.when(row == last_row)
        def _():
            greet(chan - 2, down)

        def pass_down():
            pl.semaphore_wait(down, 1)

            @pl.when(row > 0)
            def _():
                greet(chan - 2, down)

    shape = (groups, lanes)
    tile_at = iota(shape, 1) // GROUP
    part_at = iota(shape, 0) // per
    part_hops, tile_hops = doubling(split), doubling(blocks)
    spread = one_hot(iota((width, lanes), 0) % GROUP == iota((width, lanes), 1) % GROUP)

    def mode_rows(m):
        return slice(m * groups, (m + 1) * groups)

    def entry_rows(p, m):
        return pl.ds((p * modes + m) * groups, groups)

    own_group = iota((groups, width), 1) // GROUP == iota((groups, width), 0)

    def spread_rows(rows):
        for m, row_of in enumerate(rows):
            tall[mode_rows(m), :] = jnp.where(
                own_group, jnp.broadcast_to(row_of, (groups, width)), 0.0
            )
        return jnp.dot(
            tall[0 : len(rows) * groups, :],
            spread,
            precision=HIGHEST,
            preferred_element_type=jnp.float32,
        )

    def moved_to(value, p, part):
        shift = (part - p) * per % groups
        return pltpu.roll(value, shift, 0) if shift else value

    def of_piece(value, p):
        whole = moved_to(value, p, 0)
        for part in range(1, split):
            whole = jnp.where(part_at == part, moved_to(value, p, part), whole)
        return whole

    def slot_of(m):
        return m // (blocks * split), m // blocks % split, m % blocks

    def in_slot(m):
        plane, part, tile = slot_of(m)
        return jnp.logical_and(part_at == part, tile_at == tile)

    loads[1].wait()
    rate_s[...] = spread_rows([rate_ref[m : m + 1, :] for m in range(modes)])
    for m in range(modes):
        rates = rate_s[mode_rows(m), :]
        decay, far_decay = jnp.exp(-rates), jnp.exp(rates * (-float(span)))
        for p in range(split):
            powers[0, entry_rows(p, m), :] = of_piece(decay, p)
            powers[1, entry_rows(p, m), :] = of_piece(far_decay, p)

    make_bands(0)
    loads[2].wait()
    loads[3].wait()
    weights = spread_rows([residue_ref[m : m + 1, :] for m in range(modes)])
    residue_s[0 : modes * groups, :] = weights * jnp.sqrt(2.0 * rate_s[...] / modes)
    residue_s[modes * groups : (modes + 1) * groups, :] = spread_rows([skip_ref[...]])

    def late_tables():
        tile_start = (tile_at * BLOCK).astype(jnp.float32)
        packed = {}
        for m in range(modes):
            rates = rate_s[mode_rows(m), :]
            start = jnp.exp(-rates * tile_start)
            for p in range(split):
                powers[2, entry_rows(p, m), :] = of_piece(start, p)
            plane, part, tile = slot_of(m)
            packed[plane, part] = jnp.where(tile_at == tile, rates, packed.get((plane, part), rates))
        for p in range(split):
            for plane in range(planes):
                whole = jnp.zeros(shape, jnp.float32)
                for part in range(split):
                    if (plane, part) in packed:
                        placed = moved_to(packed[plane, part], p, part)
                        whole = jnp.where(part_at == part, placed, whole)
                across[p, plane * groups : (plane + 1) * groups, :] = jnp.exp(
                    whole * (-float(tokens))
                )

    late_tables()

    def short(stream, g):
        rows_of = slice(g * GROUP, (g + 1) * GROUP)
        tiles = [proj_ref[stream, rows_of, b * BLOCK : (b + 1) * BLOCK] for b in range(blocks)]
        before = [halo[stream, rows_of, :]] + tiles[:-1]
        signal = jnp.concatenate(
            [jnp.concatenate(before, axis=0), jnp.concatenate(tiles, axis=0)], axis=1
        )
        return lax.dot_general(
            bands[stream, g], signal, (((1,), (1,)), ((), ())), preferred_element_type=jnp.float32
        )

    def strided(p, part, inside):
        return pl.ds(p * span * groups + part * per + inside, span, stride=groups)

    def keep(ref, g, value):
        p, inside = g // per, g % per
        for part in range(split):
            ref[strided(p, part, inside), :] = value[part * span : (part + 1) * span]

    def step_rows(p, r):
        return pl.ds(pl.multiple_of((p * span + r) * groups, groups), groups)

    def power(k, p, m):
        return powers[k, entry_rows(p, m), :]

    zero = jnp.zeros(shape, jnp.float32)

    def end_copy(hop, p):
        return pltpu.make_async_remote_copy(
            src_ref=own_end.at[p],
            dst_ref=ends.at[hop - 1, p],
            send_sem=end_send.at[hop - 1, p],
            recv_sem=end_recv.at[hop - 1, p],
            device_id={"ctx": (index + hop) % ctx},
            device_id_type=MESH,
        )

    end_copies = {(hop, p): end_copy(hop, p) for hop in range(1, ctx) for p in range(split)}

    def first_pass(p):
        @pl.when(index > 0)
        def _():
            halo_copies[p].wait_recv()

        for g in range(p * per, (p + 1) * per):
            keep(mixed, g, short(1, g) * short(2, g))
        decay = [power(0, p, m) for m in range(modes)]

        def gather_step(r, states):
            x = mixed[step_rows(p, r), :]
            return tuple(d * s + x for d, s in zip(decay, states))

        last = lax.fori_loop(0, span, gather_step, (zero,) * modes, unroll=16)
        packed = [zero] * planes
        for m in range(modes):
            total, factor = last[m], power(1, p, m)
            for hop in part_hops:
                moved = factor * pltpu.roll(total, per * hop, 0)
                total = total + jnp.where(part_at >= hop, moved, 0.0)
                factor = factor * factor
            inner[entry_rows(p, m), :] = total
            if split > 1:
                total = jnp.where(part_at == split - 1, total, 0.0)
                for hop in part_hops:
                    total = total + pltpu.roll(total, per * hop, 0)
            for hop in tile_hops:
                moved = factor * pltpu.roll(total, GROUP * hop, 1)
                total = total + jnp.where(tile_at >= hop, moved, 0.0)
                factor = factor * factor
            outer[entry_rows(p, m), :] = total
            plane, part, tile = slot_of(m)
            placed = pltpu.roll(total, GROUP * ((tile + 1) % blocks), 1)
            packed[plane] = jnp.where(in_slot(m), placed, packed[plane])
        for plane in range(planes):
            own_end[p, plane * groups : (plane + 1) * groups, :] = packed[plane]
        for hop in range(1, ctx):

            @pl.when(index < ctx - hop)
            def _():
                end_copies[hop, p].start()

    def second_pass(p):
        for g in range(p * per, (p + 1) * per):
            keep(query, g, short(0, g))
        for m in range(modes):
            far_decay = factor = power(1, p, m)
            passed = jnp.ones(shape, jnp.float32)
            for part in range(1, split):
                passed = jnp.where(part_at == part, factor, passed)
                factor = factor * far_decay
            own = passed * jnp.where(
                tile_at >= 1, pltpu.roll(outer[entry_rows(p, m), :], GROUP, 1), 0.0
            )
            if split > 1:
                own = own + jnp.where(
                    part_at >= 1, pltpu.roll(inner[entry_rows(p, m), :], per, 0), 0.0
                )
            inner[entry_rows(p, m), :] = own
            outer[entry_rows(p, m), :] = passed * power(2, p, m)
        for hop in range(1, ctx):

            @pl.when(index >= hop)
            def _():
                end_copies[hop, p].wait_recv()

            @pl.when(index < hop)
            def _():
                ends[hop - 1, p] = jnp.zeros(ends.shape[2:], jnp.float32)

        arrived = []
        for plane in range(planes):
            rows = slice(plane * groups, (plane + 1) * groups)
            total = zero
            for hop in range(ctx - 1, 0, -1):
                total = across[p, rows, :] * total + ends[hop - 1, p, rows, :]
            arrived.append(total)
        entry = []
        for m in range(modes):
            incoming = jnp.where(in_slot(m), arrived[slot_of(m)[0]], 0.0)
            for hop in part_hops:
                incoming = incoming + pltpu.roll(incoming, per * hop, 0)
            for hop in tile_hops:
                incoming = incoming + pltpu.roll(incoming, GROUP * hop, 1)
            entry.append(inner[entry_rows(p, m), :] + outer[entry_rows(p, m), :] * incoming)
        decay = [power(0, p, m) for m in range(modes)]
        weight = [of_piece(residue_s[mode_rows(m), :], p) for m in range(modes)]
        skip = of_piece(residue_s[mode_rows(modes), :], p)

        def step(r, states):
            where = step_rows(p, r)
            x = mixed[where, :]
            new = tuple(d * s + x for d, s in zip(decay, states))
            terms = [w * s for w, s in zip(weight, new)] + [skip * x]
            while len(terms) > 1:
                terms = [a + b for a, b in zip(terms[::2], terms[1::2])] + (
                    [terms[-1]] if len(terms) % 2 else []
                )
            work[where, :] = query[where, :] * terms[0]
            return new

        lax.fori_loop(0, span, step, tuple(entry), unroll=8)

    def turn(p, put):
        for inside in range(per):
            rows = [work[strided(p, part, inside), :] for part in range(split)]
            whole = jnp.concatenate(rows, axis=0) if split > 1 else rows[0]
            turned = whole.astype(jnp.bfloat16).T
            for b in range(blocks):
                put(p * per + inside, b, turned[b * GROUP : (b + 1) * GROUP])

    for p in range(split):
        first_pass(p)
    if swap:

        @pl.when(row > 0)
        def _():
            pl.semaphore_wait(up, 1)

        @pl.when(jnp.logical_and(row > 0, row < last_row))
        def _():
            greet(chan + 2, up)

        pl.when(jnp.logical_and(row > last_row // 2, row < last_row))(pass_down)

    @pl.when(index > 0)
    def _():
        halo_copies[split].wait_recv()

    if swap:
        there = []

        def put(g, b, tile):
            parts[b, g * GROUP : (g + 1) * GROUP, :] = tile

        for p in range(split):
            second_pass(p)
            turn(p, put)
            if p == 0:
                pl.when(row <= last_row // 2)(pass_down)
            rows = pl.ds(p * half, half)
            for mask in range(chans - 1, 0, -1):
                peer = flipped(chan, mask)
                there.append(
                    pltpu.make_async_remote_copy(
                        src_ref=parts.at[peer, rows],
                        dst_ref=gath.at[chan, rows],
                        send_sem=there_send.at[p, mask - 1],
                        recv_sem=there_recv.at[p, mask - 1],
                        device_id={"chan": peer},
                        device_id_type=MESH,
                    )
                )
                there[-1].start()
        exchange(
            chans,
            chan,
            gath,
            own_weight,
            weight_copy,
            out_ref,
            parts,
            turned_weight,
            results,
            there,
            back_send,
            back_recv,
        )
    else:
        per_piece = blocks // PIECES

        def put(g, b, tile):
            inside = (b % per_piece) * BLOCK
            gath[
                chan, b // per_piece, g * GROUP : (g + 1) * GROUP, inside : inside + BLOCK
            ] = tile

        for p in range(split):
            second_pass(p)
            turn(p, put)
        ring(chans, chan, place, left, right, gath, own_weight, weight_copy, out_ref, *rest)

    @pl.when(index < ctx - 1)
    def _():
        for copy in halo_copies:
            copy.wait_send()

    for hop in range(1, ctx):

        @pl.when(index < ctx - hop)
        def _():
            for p in range(split):
                end_copies[hop, p].wait_send()


def per_device(ctx, chans, proj, taps, rate, residue, skip, out_weight):
    width, tokens = proj.shape[1:]
    modes = rate.shape[1]
    groups, blocks = width // GROUP, tokens // BLOCK
    lanes = blocks * GROUP
    split = split_of(groups)
    planes = -(-modes // (blocks * split))
    swap = is_swap(chans, width, tokens)
    if width % 128:
        out_weight = lax.dynamic_slice_in_dim(
            out_weight, lax.axis_index("chan") * width, width, 1
        )
    vmem = pl.BlockSpec(memory_space=pltpu.VMEM)
    if swap:
        blocks_of = pltpu.VMEM((chans, width, BLOCK), jnp.bfloat16)
        square = pltpu.VMEM(out_weight.shape, jnp.bfloat16)
        several = pltpu.SemaphoreType.DMA((chans - 1,))
        by_part = pltpu.SemaphoreType.DMA((split, chans - 1))
        weight_scratch, gath_scratch = square, blocks_of
        rest = [blocks_of, square, blocks_of, by_part, by_part, several, several]
    else:
        weight_scratch = pltpu.VMEM((chans * width, width), jnp.bfloat16)
        gath_scratch = pltpu.VMEM((chans, PIECES, width, tokens // PIECES), jnp.bfloat16)
        hops = pltpu.SemaphoreType.DMA((2, chans // 2, PIECES))
        rest = [pltpu.VMEM((PIECES, width, tokens // PIECES), jnp.float32), hops, hops]
    major = pltpu.VMEM((BLOCK * groups, lanes), jnp.float32)
    rows = split * modes * groups
    table = pltpu.VMEM((rows, lanes), jnp.float32)
    packed = (split, planes * groups, lanes)
    return pl.pallas_call(
        functools.partial(fused, ctx, chans),
        out_shape=pltpu.VMEM((width, tokens), jnp.bfloat16),
        in_specs=[pl.BlockSpec(memory_space=pltpu.HBM)] * 6,
        out_specs=vmem,
        scratch_shapes=[
            pltpu.VMEM(proj.shape, proj.dtype),
            pltpu.VMEM(taps.shape, taps.dtype),
            pltpu.VMEM((modes, width), jnp.float32),
            pltpu.VMEM((modes, width), jnp.float32),
            pltpu.VMEM((1, width), jnp.float32),
            pltpu.VMEM((3, width, BLOCK), jnp.bfloat16),
            major,
            major,
            major,
            pltpu.VMEM((3, groups, BLOCK, 2 * BLOCK), jnp.bfloat16),
            pltpu.VMEM((modes * groups, width), jnp.float32),
            pltpu.VMEM((modes * groups, lanes), jnp.float32),
            pltpu.VMEM(((modes + 1) * groups, lanes), jnp.float32),
            pltpu.VMEM((3, rows, lanes), jnp.float32),
            pltpu.VMEM(packed, jnp.float32),
            table,
            table,
            pltpu.VMEM(packed, jnp.float32),
            pltpu.VMEM((ctx - 1, *packed), jnp.float32),
            weight_scratch,
            gath_scratch,
            pltpu.SemaphoreType.DMA,
            pltpu.SemaphoreType.DMA((5,)),
            pltpu.SemaphoreType.DMA((2 * (split + 1),)),
            pltpu.SemaphoreType.DMA((ctx - 1, split)),
            pltpu.SemaphoreType.DMA((ctx - 1, split)),
            pltpu.SemaphoreType.REGULAR((2,)),
            *rest,
        ],
        compiler_params=pltpu.CompilerParams(
            vmem_limit_bytes=58 << 20, collective_id=0, has_side_effects=True
        ),
        name="fused",
    )(proj, taps, rate.T, residue.T, skip.reshape(1, width), out_weight)


def solution(mesh):
    in_specs = (P(None, "chan", "ctx"), P(), P("chan", None), P("chan", None), P("chan"), P())
    out_specs = P("chan", "ctx")
    return jax.shard_map(
        functools.partial(per_device, mesh.shape["ctx"], mesh.shape["chan"]),
        mesh=mesh,
        in_specs=in_specs,
        out_specs=out_specs,
        check_vma=False,
    )
```

```python
import functools
import jax
import jax.numpy as jnp
from jax import lax
from jax.experimental import pallas as pl
from jax.experimental.pallas import tpu as pltpu
from jax.sharding import PartitionSpec as P

GROUP = 16
BLOCK = 128
PIECES = 4
SPLIT = 2
OWN = 0
MESH = pl.DeviceIdType.MESH
HIGHEST = lax.Precision.HIGHEST


def iota(shape, axis):
    return lax.broadcasted_iota(jnp.int32, shape, axis)


def one_hot(hit, dtype=jnp.float32):
    return hit.astype(jnp.float32).astype(dtype)


def ring_place(chan, n):
    row, side = chan // 2, chan % 2
    return row + side * (n - 1 - 2 * row)


def ring_chan(place, n):
    side = place // (n // 2)
    row = place + side * (n - 1 - 2 * place)
    return 2 * row + side


def exchange(
    chans,
    chan,
    gath,
    weight,
    weight_copy,
    out_ref,
    parts,
    turned_weight,
    results,
    there,
    back_send,
    back_recv,
):
    width = out_ref.shape[0]
    gath[chan] = parts[chan]
    weight_copy.wait()
    turned_weight[...] = weight[...].T
    for copy in there:
        copy.wait_recv()
    everything = gath[...].reshape(chans * width, BLOCK)

    def project(shard):
        rows_of = pl.ds(pl.multiple_of(shard * width, width), width)
        return jnp.dot(
            turned_weight[rows_of, :], everything, preferred_element_type=jnp.float32
        ).astype(jnp.bfloat16)

    own_columns = pl.ds(pl.multiple_of(chan * BLOCK, BLOCK), BLOCK)
    back = []
    row = chan // 2
    beside = row + 1 - 2 * (row % 2)
    for mask in masks_of(chan, chans, (1, OWN, 3, 2), (row, 1, OWN, beside)):
        peer = flipped_by(chan, chans, mask)
        results[mask - 1] = project(peer)
        back.append(
            pltpu.make_async_remote_copy(
                src_ref=results.at[mask - 1],
                dst_ref=out_ref.at[:, own_columns],
                send_sem=back_send.at[mask - 1],
                recv_sem=back_recv.at[mask - 1],
                device_id={"chan": peer},
                device_id_type=MESH,
            )
        )
        back[-1].start()
    out_ref[:, own_columns] = project(chan)
    for copy in back:
        copy.wait_recv()
    for copy in there + back:
        copy.wait_send()


def ring(
    chans,
    chan,
    place,
    left,
    right,
    gath,
    own_weight,
    weight_copy,
    out_ref,
    acc,
    ring_send,
    ring_recv,
):
    width, tokens = out_ref.shape
    cols = tokens // PIECES
    half = chans // 2

    def ring_copy(way, hop, piece):
        shard = ring_chan((place + chans + (-hop if way == 0 else hop)) % chans, chans)
        return pltpu.make_async_remote_copy(
            src_ref=gath.at[shard, piece],
            dst_ref=gath.at[shard, piece],
            send_sem=ring_send.at[way, hop, piece],
            recv_sem=ring_recv.at[way, hop, piece],
            device_id={"chan": right if way == 0 else left},
            device_id_type=MESH,
        )

    def travels(way, hop, piece):
        if hop < half - 1:
            return True
        return hop == half - 1 and (piece < PIECES // 2) == (way == 0)

    copies = {}
    for piece in range(PIECES):
        for way in range(2):
            copies[way, 0, piece] = ring_copy(way, 0, piece)
            copies[way, 0, piece].start()
    weight_copy.wait()

    def project(shard, piece):
        rows_of = pl.ds(pl.multiple_of(shard * width, width), width)
        return lax.dot_general(
            own_weight[rows_of, :],
            gath[shard, piece],
            (((0,), (0,)), ((), ())),
            preferred_element_type=jnp.float32,
        )

    for piece in range(PIECES):
        acc[piece] = project(chan, piece)
    for hop in range(1, half + 1):
        for piece in range(PIECES):
            arrived = []
            for way in range(2):
                if not travels(way, hop - 1, piece):
                    continue
                copies[way, hop - 1, piece].wait_recv()
                if travels(way, hop, piece):
                    copies[way, hop, piece] = ring_copy(way, hop, piece)
                    copies[way, hop, piece].start()
                arrived.append(
                    ring_chan((place + chans + (-hop if way == 0 else hop)) % chans, chans)
                )
            total = acc[piece]
            for shard in arrived:
                total = total + project(shard, piece)
            if hop == half:
                out_ref[:, piece * cols : (piece + 1) * cols] = total.astype(out_ref.dtype)
            else:
                acc[piece] = total

    for key in copies:
        copies[key].wait_send()


def flipped_by(chan, chans, mask):
    peer, bit = chan, 1
    while bit < chans:
        peer = peer + bit * (mask // bit % 2) * (1 - 2 * (chan // bit % 2))
        bit *= 2
    return peer


def row_pairs(*flips):
    return [(flip, side) for flip in flips for side in (1, 0) if side or flip is not OWN]


def masks_of(chan, chans, near, far):
    is_far = chan // (chans // 2)
    return [
        2 * (a + is_far * (c - a)) + b + is_far * (d - b)
        for (a, b), (c, d) in zip(row_pairs(*near), row_pairs(*far))
    ]


def greet(peer, sem):
    pl.semaphore_signal(sem, inc=1, device_id={"chan": peer}, device_id_type=MESH)


def is_swap(chans, width, tokens):
    return chans == 8 and width == BLOCK and tokens == chans * BLOCK


def split_of(groups):
    split = 1
    while split < SPLIT and groups % (2 * split) == 0:
        split *= 2
    return split


def doubling(end):
    hops = [1]
    while hops[-1] * 2 < end:
        hops.append(hops[-1] * 2)
    return hops if end > 1 else []


def fused(
    ctx,
    chans,
    proj_in,
    taps_in,
    rate_in,
    residue_in,
    skip_in,
    weight_ref,
    out_ref,
    proj_ref,
    taps_ref,
    rate_ref,
    residue_ref,
    skip_ref,
    halo,
    query,
    mixed,
    work,
    bands,
    tall,
    rate_s,
    residue_s,
    powers,
    across,
    inner,
    outer,
    own_end,
    ends,
    own_weight,
    gath,
    weight_sem,
    load_sems,
    halo_sems,
    end_send,
    end_recv,
    meet_sems,
    *rest,
):
    width, tokens = proj_ref.shape[1:]
    modes = rate_ref.shape[0]
    groups, blocks = width // GROUP, tokens // BLOCK
    lanes = blocks * GROUP
    split = split_of(groups)
    per, span, half = groups // split, BLOCK // split, width // split
    planes = own_end.shape[1] // groups
    swap = is_swap(chans, width, tokens)
    index = lax.axis_index("ctx")
    chan = lax.axis_index("chan")
    if swap:
        row, last_row = chan // 2, chans // 2 - 1
        peers = [(chan + 1 - 2 * (chan % 2), None), (chan - 2, row > 0), (chan + 2, row < last_row)]
        parts, turned_weight, results, there_send, there_recv, back_send, back_recv = rest
    else:
        place = ring_place(chan, chans)
        right = ring_chan((place + 1) % chans, chans)
        left = ring_chan((place + chans - 1) % chans, chans)
        peers = [(left, None), (right, None)]

    barrier = pltpu.get_barrier_semaphore()
    for hop in range(1, ctx):
        pl.semaphore_signal(
            barrier, inc=1, device_id={"ctx": (index + hop) % ctx}, device_id_type=MESH
        )
    expected = ctx - 1
    for peer, there_is in peers:
        if there_is is None:
            greet(peer, barrier)
            expected = expected + 1
        else:
            pl.when(there_is)(functools.partial(greet, peer, barrier))
            expected = expected + jnp.where(there_is, 1, 0)

    loads = [
        pltpu.make_async_copy(source, target, load_sems.at[k])
        for k, (source, target) in enumerate(
            (
                (taps_in, taps_ref),
                (rate_in, rate_ref),
                (residue_in, residue_ref),
                (skip_in, skip_ref),
                (proj_in, proj_ref),
            )
        )
    ]
    for load in loads:
        load.start()
    if swap or weight_ref.shape[1] == width:
        weight_from = weight_ref
    else:
        weight_from = weight_ref.at[:, pl.ds(pl.multiple_of(chan * width, width), width)]
    weight_copy = pltpu.make_async_copy(weight_from, own_weight, weight_sem)

    loads[0].wait()
    all_groups = taps_ref.shape[1]
    pick = one_hot(
        iota((groups, all_groups), 1) == iota((groups, all_groups), 0) + chan * groups,
        jnp.bfloat16,
    )
    flip = one_hot(
        iota((BLOCK, 2 * BLOCK), 1) == BLOCK - iota((BLOCK, 2 * BLOCK), 0), jnp.bfloat16
    )

    def make_bands(stream):
        own = jnp.dot(pick, taps_ref[stream], preferred_element_type=jnp.float32)
        rows = jnp.dot(own.astype(jnp.bfloat16), flip, preferred_element_type=jnp.float32)
        for g in range(groups):
            wide = jnp.broadcast_to(rows[g : g + 1, :], (BLOCK, 2 * BLOCK))
            bands[stream, g] = pltpu.roll(wide, 0, 1, stride=1, stride_axis=0).astype(
                jnp.bfloat16
            )

    make_bands(1)
    make_bands(2)

    loads[4].wait()
    pl.semaphore_wait(barrier, expected)
    halo_parts = [(pl.ds(1, 2), pl.ds(p * half, half)) for p in range(split)]
    halo_parts.append((pl.ds(0, 1), pl.ds(0, width)))
    halo_copies = [
        pltpu.make_async_remote_copy(
            src_ref=proj_ref.at[streams, rows, pl.ds(tokens - BLOCK, BLOCK)],
            dst_ref=halo.at[streams, rows],
            send_sem=halo_sems.at[2 * k],
            recv_sem=halo_sems.at[2 * k + 1],
            device_id={"ctx": (index + 1) % ctx},
            device_id_type=MESH,
        )
        for k, (streams, rows) in enumerate(halo_parts)
    ]

    @pl.when(index < ctx - 1)
    def _():
        for copy in halo_copies:
            copy.start()

    @pl.when(index == 0)
    def _():
        halo[...] = jnp.zeros_like(halo)

    weight_copy.start()

    if swap:
        up, down = meet_sems.at[0], meet_sems.at[1]

        @pl.when(row == 0)
        def _():
            greet(chan + 2, up)

        @pl.when(row == last_row)
        def _():
            greet(chan - 2, down)

        def pass_down():
            pl.semaphore_wait(down, 1)

            @pl.when(row > 0)
            def _():
                greet(chan - 2, down)

    shape = (groups, lanes)
    tile_at = iota(shape, 1) // GROUP
    part_at = iota(shape, 0) // per
    part_hops, tile_hops = doubling(split), doubling(blocks)
    spread = one_hot(iota((width, lanes), 0) % GROUP == iota((width, lanes), 1) % GROUP)

    def mode_rows(m):
        return slice(m * groups, (m + 1) * groups)

    def entry_rows(p, m):
        return pl.ds((p * modes + m) * groups, groups)

    own_group = iota((groups, width), 1) // GROUP == iota((groups, width), 0)

    def spread_rows(rows):
        for m, row_of in enumerate(rows):
            tall[mode_rows(m), :] = jnp.where(
                own_group, jnp.broadcast_to(row_of, (groups, width)), 0.0
            )
        return jnp.dot(
            tall[0 : len(rows) * groups, :],
            spread,
            precision=HIGHEST,
            preferred_element_type=jnp.float32,
        )

    def moved_to(value, p, part):
        shift = (part - p) * per % groups
        return pltpu.roll(value, shift, 0) if shift else value

    def of_piece(value, p):
        whole = moved_to(value, p, 0)
        for part in range(1, split):
            whole = jnp.where(part_at == part, moved_to(value, p, part), whole)
        return whole

    def slot_of(m):
        return m // (blocks * split), m // blocks % split, m % blocks

    def in_slot(m):
        plane, part, tile = slot_of(m)
        return jnp.logical_and(part_at == part, tile_at == tile)

    loads[1].wait()
    rate_s[...] = spread_rows([rate_ref[m : m + 1, :] for m in range(modes)])
    for m in range(modes):
        rates = rate_s[mode_rows(m), :]
        decay, far_decay = jnp.exp(-rates), jnp.exp(rates * (-float(span)))
        for p in range(split):
            powers[0, entry_rows(p, m), :] = of_piece(decay, p)
            powers[1, entry_rows(p, m), :] = of_piece(far_decay, p)

    make_bands(0)
    loads[2].wait()
    loads[3].wait()
    weights = spread_rows([residue_ref[m : m + 1, :] for m in range(modes)])
    residue_s[0 : modes * groups, :] = weights * jnp.sqrt(2.0 * rate_s[...] / modes)
    residue_s[modes * groups : (modes + 1) * groups, :] = spread_rows([skip_ref[...]])

    def late_tables():
        tile_start = (tile_at * BLOCK).astype(jnp.float32)
        packed = {}
        for m in range(modes):
            rates = rate_s[mode_rows(m), :]
            start = jnp.exp(-rates * tile_start)
            for p in range(split):
                powers[2, entry_rows(p, m), :] = of_piece(start, p)
            plane, part, tile = slot_of(m)
            packed[plane, part] = jnp.where(tile_at == tile, rates, packed.get((plane, part), rates))
        for p in range(split):
            for plane in range(planes):
                whole = jnp.zeros(shape, jnp.float32)
                for part in range(split):
                    if (plane, part) in packed:
                        placed = moved_to(packed[plane, part], p, part)
                        whole = jnp.where(part_at == part, placed, whole)
                across[p, plane * groups : (plane + 1) * groups, :] = jnp.exp(
                    whole * (-float(tokens))
                )

    late_tables()

    def short(stream, g):
        rows_of = slice(g * GROUP, (g + 1) * GROUP)
        tiles = [proj_ref[stream, rows_of, b * BLOCK : (b + 1) * BLOCK] for b in range(blocks)]
        before = [halo[stream, rows_of, :]] + tiles[:-1]
        signal = jnp.concatenate(
            [jnp.concatenate(before, axis=0), jnp.concatenate(tiles, axis=0)], axis=1
        )
        return lax.dot_general(
            bands[stream, g], signal, (((1,), (1,)), ((), ())), preferred_element_type=jnp.float32
        )

    def strided(p, part, inside):
        return pl.ds(p * span * groups + part * per + inside, span, stride=groups)

    def keep(ref, g, value):
        p, inside = g // per, g % per
        for part in range(split):
            ref[strided(p, part, inside), :] = value[part * span : (part + 1) * span]

    def step_rows(p, r):
        return pl.ds(pl.multiple_of((p * span + r) * groups, groups), groups)

    def power(k, p, m):
        return powers[k, entry_rows(p, m), :]

    zero = jnp.zeros(shape, jnp.float32)

    def end_copy(hop, p):
        return pltpu.make_async_remote_copy(
            src_ref=own_end.at[p],
            dst_ref=ends.at[hop - 1, p],
            send_sem=end_send.at[hop - 1, p],
            recv_sem=end_recv.at[hop - 1, p],
            device_id={"ctx": (index + hop) % ctx},
            device_id_type=MESH,
        )

    end_copies = {(hop, p): end_copy(hop, p) for hop in range(1, ctx) for p in range(split)}

    def first_pass(p):
        @pl.when(index > 0)
        def _():
            halo_copies[p].wait_recv()

        for g in range(p * per, (p + 1) * per):
            keep(mixed, g, short(1, g) * short(2, g))
        decay = [power(0, p, m) for m in range(modes)]

        def gather_step(r, states):
            x = mixed[step_rows(p, r), :]
            return tuple(d * s + x for d, s in zip(decay, states))

        last = lax.fori_loop(0, span, gather_step, (zero,) * modes, unroll=16)
        packed = [zero] * planes
        for m in range(modes):
            total, factor = last[m], power(1, p, m)
            for hop in part_hops:
                moved = factor * pltpu.roll(total, per * hop, 0)
                total = total + jnp.where(part_at >= hop, moved, 0.0)
                factor = factor * factor
            inner[entry_rows(p, m), :] = total
            if split > 1:
                total = jnp.where(part_at == split - 1, total, 0.0)
                for hop in part_hops:
                    total = total + pltpu.roll(total, per * hop, 0)
            for hop in tile_hops:
                moved = factor * pltpu.roll(total, GROUP * hop, 1)
                total = total + jnp.where(tile_at >= hop, moved, 0.0)
                factor = factor * factor
            outer[entry_rows(p, m), :] = total
            plane, part, tile = slot_of(m)
            placed = pltpu.roll(total, GROUP * ((tile + 1) % blocks), 1)
            packed[plane] = jnp.where(in_slot(m), placed, packed[plane])
        for plane in range(planes):
            own_end[p, plane * groups : (plane + 1) * groups, :] = packed[plane]
        for hop in range(1, ctx):

            @pl.when(index < ctx - hop)
            def _():
                end_copies[hop, p].start()

    def second_pass(p):
        for g in range(p * per, (p + 1) * per):
            keep(query, g, short(0, g))
        for m in range(modes):
            far_decay = factor = power(1, p, m)
            passed = jnp.ones(shape, jnp.float32)
            for part in range(1, split):
                passed = jnp.where(part_at == part, factor, passed)
                factor = factor * far_decay
            own = passed * jnp.where(
                tile_at >= 1, pltpu.roll(outer[entry_rows(p, m), :], GROUP, 1), 0.0
            )
            if split > 1:
                own = own + jnp.where(
                    part_at >= 1, pltpu.roll(inner[entry_rows(p, m), :], per, 0), 0.0
                )
            inner[entry_rows(p, m), :] = own
            outer[entry_rows(p, m), :] = passed * power(2, p, m)
        for hop in range(1, ctx):

            @pl.when(index >= hop)
            def _():
                end_copies[hop, p].wait_recv()

            @pl.when(index < hop)
            def _():
                ends[hop - 1, p] = jnp.zeros(ends.shape[2:], jnp.float32)

        arrived = []
        for plane in range(planes):
            rows = slice(plane * groups, (plane + 1) * groups)
            total = zero
            for hop in range(ctx - 1, 0, -1):
                total = across[p, rows, :] * total + ends[hop - 1, p, rows, :]
            arrived.append(total)
        entry = []
        for m in range(modes):
            incoming = jnp.where(in_slot(m), arrived[slot_of(m)[0]], 0.0)
            for hop in part_hops:
                incoming = incoming + pltpu.roll(incoming, per * hop, 0)
            for hop in tile_hops:
                incoming = incoming + pltpu.roll(incoming, GROUP * hop, 1)
            entry.append(inner[entry_rows(p, m), :] + outer[entry_rows(p, m), :] * incoming)
        decay = [power(0, p, m) for m in range(modes)]
        weight = [of_piece(residue_s[mode_rows(m), :], p) for m in range(modes)]
        skip = of_piece(residue_s[mode_rows(modes), :], p)

        def step(r, states):
            where = step_rows(p, r)
            x = mixed[where, :]
            new = tuple(d * s + x for d, s in zip(decay, states))
            terms = [w * s for w, s in zip(weight, new)] + [skip * x]
            while len(terms) > 1:
                terms = [a + b for a, b in zip(terms[::2], terms[1::2])] + (
                    [terms[-1]] if len(terms) % 2 else []
                )
            work[where, :] = query[where, :] * terms[0]
            return new

        lax.fori_loop(0, span, step, tuple(entry), unroll=8)

    def turn(p, put):
        for inside in range(per):
            rows = [work[strided(p, part, inside), :] for part in range(split)]
            whole = jnp.concatenate(rows, axis=0) if split > 1 else rows[0]
            turned = whole.astype(jnp.bfloat16).T
            for b in range(blocks):
                put(p * per + inside, b, turned[b * GROUP : (b + 1) * GROUP])

    for p in range(split):
        first_pass(p)
    if swap:

        @pl.when(row > 0)
        def _():
            pl.semaphore_wait(up, 1)

        @pl.when(jnp.logical_and(row > 0, row < last_row))
        def _():
            greet(chan + 2, up)

        pl.when(jnp.logical_and(row > last_row // 2, row < last_row))(pass_down)

    @pl.when(index > 0)
    def _():
        halo_copies[split].wait_recv()

    if swap:
        there = []

        def put(g, b, tile):
            parts[b, g * GROUP : (g + 1) * GROUP, :] = tile

        for p in range(split):
            second_pass(p)
            turn(p, put)
            if p == 0:
                pl.when(row <= last_row // 2)(pass_down)
            rows = pl.ds(p * half, half)
            beside = row + 1 - 2 * (row % 2)
            for mask in masks_of(chan, chans, (3, 2, 1, OWN), (1, OWN, row, beside)):
                peer = flipped_by(chan, chans, mask)
                there.append(
                    pltpu.make_async_remote_copy(
                        src_ref=parts.at[peer, rows],
                        dst_ref=gath.at[chan, rows],
                        send_sem=there_send.at[p, mask - 1],
                        recv_sem=there_recv.at[p, mask - 1],
                        device_id={"chan": peer},
                        device_id_type=MESH,
                    )
                )
                there[-1].start()
        exchange(
            chans,
            chan,
            gath,
            own_weight,
            weight_copy,
            out_ref,
            parts,
            turned_weight,
            results,
            there,
            back_send,
            back_recv,
        )
    else:
        per_piece = blocks // PIECES

        def put(g, b, tile):
            inside = (b % per_piece) * BLOCK
            gath[
                chan, b // per_piece, g * GROUP : (g + 1) * GROUP, inside : inside + BLOCK
            ] = tile

        for p in range(split):
            second_pass(p)
            turn(p, put)
        ring(chans, chan, place, left, right, gath, own_weight, weight_copy, out_ref, *rest)

    @pl.when(index < ctx - 1)
    def _():
        for copy in halo_copies:
            copy.wait_send()

    for hop in range(1, ctx):

        @pl.when(index < ctx - hop)
        def _():
            for p in range(split):
                end_copies[hop, p].wait_send()


def per_device(ctx, chans, proj, taps, rate, residue, skip, out_weight):
    width, tokens = proj.shape[1:]
    modes = rate.shape[1]
    groups, blocks = width // GROUP, tokens // BLOCK
    lanes = blocks * GROUP
    split = split_of(groups)
    planes = -(-modes // (blocks * split))
    swap = is_swap(chans, width, tokens)
    if width % 128:
        out_weight = lax.dynamic_slice_in_dim(
            out_weight, lax.axis_index("chan") * width, width, 1
        )
    vmem = pl.BlockSpec(memory_space=pltpu.VMEM)
    if swap:
        blocks_of = pltpu.VMEM((chans, width, BLOCK), jnp.bfloat16)
        square = pltpu.VMEM(out_weight.shape, jnp.bfloat16)
        several = pltpu.SemaphoreType.DMA((chans - 1,))
        by_part = pltpu.SemaphoreType.DMA((split, chans - 1))
        weight_scratch, gath_scratch = square, blocks_of
        rest = [blocks_of, square, blocks_of, by_part, by_part, several, several]
    else:
        weight_scratch = pltpu.VMEM((chans * width, width), jnp.bfloat16)
        gath_scratch = pltpu.VMEM((chans, PIECES, width, tokens // PIECES), jnp.bfloat16)
        hops = pltpu.SemaphoreType.DMA((2, chans // 2, PIECES))
        rest = [pltpu.VMEM((PIECES, width, tokens // PIECES), jnp.float32), hops, hops]
    major = pltpu.VMEM((BLOCK * groups, lanes), jnp.float32)
    rows = split * modes * groups
    table = pltpu.VMEM((rows, lanes), jnp.float32)
    packed = (split, planes * groups, lanes)
    return pl.pallas_call(
        functools.partial(fused, ctx, chans),
        out_shape=pltpu.VMEM((width, tokens), jnp.bfloat16),
        in_specs=[pl.BlockSpec(memory_space=pltpu.HBM)] * 6,
        out_specs=vmem,
        scratch_shapes=[
            pltpu.VMEM(proj.shape, proj.dtype),
            pltpu.VMEM(taps.shape, taps.dtype),
            pltpu.VMEM((modes, width), jnp.float32),
            pltpu.VMEM((modes, width), jnp.float32),
            pltpu.VMEM((1, width), jnp.float32),
            pltpu.VMEM((3, width, BLOCK), jnp.bfloat16),
            major,
            major,
            major,
            pltpu.VMEM((3, groups, BLOCK, 2 * BLOCK), jnp.bfloat16),
            pltpu.VMEM((modes * groups, width), jnp.float32),
            pltpu.VMEM((modes * groups, lanes), jnp.float32),
            pltpu.VMEM(((modes + 1) * groups, lanes), jnp.float32),
            pltpu.VMEM((3, rows, lanes), jnp.float32),
            pltpu.VMEM(packed, jnp.float32),
            table,
            table,
            pltpu.VMEM(packed, jnp.float32),
            pltpu.VMEM((ctx - 1, *packed), jnp.float32),
            weight_scratch,
            gath_scratch,
            pltpu.SemaphoreType.DMA,
            pltpu.SemaphoreType.DMA((5,)),
            pltpu.SemaphoreType.DMA((2 * (split + 1),)),
            pltpu.SemaphoreType.DMA((ctx - 1, split)),
            pltpu.SemaphoreType.DMA((ctx - 1, split)),
            pltpu.SemaphoreType.REGULAR((2,)),
            *rest,
        ],
        compiler_params=pltpu.CompilerParams(
            vmem_limit_bytes=58 << 20, collective_id=0, has_side_effects=True
        ),
        name="fused",
    )(proj, taps, rate.T, residue.T, skip.reshape(1, width), out_weight)


def solution(mesh):
    in_specs = (P(None, "chan", "ctx"), P(), P("chan", None), P("chan", None), P("chan"), P())
    out_specs = P("chan", "ctx")
    return jax.shard_map(
        functools.partial(per_device, mesh.shape["ctx"], mesh.shape["chan"]),
        mesh=mesh,
        in_specs=in_specs,
        out_specs=out_specs,
        check_vma=False,
    )
```

```python
import functools
import jax
import jax.numpy as jnp
from jax import lax
from jax.experimental import pallas as pl
from jax.experimental.pallas import tpu as pltpu
from jax.sharding import PartitionSpec as P

GROUP = 16
BLOCK = 128
PIECES = 4
OWN = 0
MESH = pl.DeviceIdType.MESH
HIGHEST = lax.Precision.HIGHEST


def iota(shape, axis):
    return lax.broadcasted_iota(jnp.int32, shape, axis)


def one_hot(hit, dtype=jnp.float32):
    return hit.astype(jnp.float32).astype(dtype)


def ring_place(chan, n):
    row, side = chan // 2, chan % 2
    return row + side * (n - 1 - 2 * row)


def ring_chan(place, n):
    side = place // (n // 2)
    row = place + side * (n - 1 - 2 * place)
    return 2 * row + side


def exchange(
    chans,
    chan,
    gath,
    weight,
    weight_copy,
    out_ref,
    parts,
    turned_weight,
    results,
    there,
    back_send,
    back_recv,
):
    width = out_ref.shape[0]
    gath[chan] = parts[chan]
    weight_copy.wait()
    turned_weight[...] = weight[...].T
    for copy in there:
        copy.wait_recv()
    everything = gath[...].reshape(chans * width, BLOCK)

    def project(shard):
        rows_of = pl.ds(pl.multiple_of(shard * width, width), width)
        return jnp.dot(
            turned_weight[rows_of, :], everything, preferred_element_type=jnp.float32
        ).astype(jnp.bfloat16)

    own_columns = pl.ds(pl.multiple_of(chan * BLOCK, BLOCK), BLOCK)
    back = []
    row = chan // 2
    beside = row + 1 - 2 * (row % 2)
    for mask in masks_of(chan, chans, (1, OWN, 3, 2), (row, 1, OWN, beside)):
        peer = flipped_by(chan, chans, mask)
        results[mask - 1] = project(peer)
        back.append(
            pltpu.make_async_remote_copy(
                src_ref=results.at[mask - 1],
                dst_ref=out_ref.at[:, own_columns],
                send_sem=back_send.at[mask - 1],
                recv_sem=back_recv.at[mask - 1],
                device_id={"chan": peer},
                device_id_type=MESH,
            )
        )
        back[-1].start()
    out_ref[:, own_columns] = project(chan)
    for copy in back:
        copy.wait_recv()
    for copy in there + back:
        copy.wait_send()


def ring(
    chans,
    chan,
    place,
    left,
    right,
    gath,
    own_weight,
    weight_copy,
    out_ref,
    acc,
    ring_send,
    ring_recv,
):
    width, tokens = out_ref.shape
    cols = tokens // PIECES
    half = chans // 2

    def ring_copy(way, hop, piece):
        shard = ring_chan((place + chans + (-hop if way == 0 else hop)) % chans, chans)
        return pltpu.make_async_remote_copy(
            src_ref=gath.at[shard, piece],
            dst_ref=gath.at[shard, piece],
            send_sem=ring_send.at[way, hop, piece],
            recv_sem=ring_recv.at[way, hop, piece],
            device_id={"chan": right if way == 0 else left},
            device_id_type=MESH,
        )

    def travels(way, hop, piece):
        if hop < half - 1:
            return True
        return hop == half - 1 and (piece < PIECES // 2) == (way == 0)

    copies = {}
    for piece in range(PIECES):
        for way in range(2):
            copies[way, 0, piece] = ring_copy(way, 0, piece)
            copies[way, 0, piece].start()
    weight_copy.wait()

    def project(shard, piece):
        rows_of = pl.ds(pl.multiple_of(shard * width, width), width)
        return lax.dot_general(
            own_weight[rows_of, :],
            gath[shard, piece],
            (((0,), (0,)), ((), ())),
            preferred_element_type=jnp.float32,
        )

    for piece in range(PIECES):
        acc[piece] = project(chan, piece)
    for hop in range(1, half + 1):
        for piece in range(PIECES):
            arrived = []
            for way in range(2):
                if not travels(way, hop - 1, piece):
                    continue
                copies[way, hop - 1, piece].wait_recv()
                if travels(way, hop, piece):
                    copies[way, hop, piece] = ring_copy(way, hop, piece)
                    copies[way, hop, piece].start()
                arrived.append(
                    ring_chan((place + chans + (-hop if way == 0 else hop)) % chans, chans)
                )
            total = acc[piece]
            for shard in arrived:
                total = total + project(shard, piece)
            if hop == half:
                out_ref[:, piece * cols : (piece + 1) * cols] = total.astype(out_ref.dtype)
            else:
                acc[piece] = total

    for key in copies:
        copies[key].wait_send()


def flipped_by(chan, chans, mask):
    peer, bit = chan, 1
    while bit < chans:
        peer = peer + bit * (mask // bit % 2) * (1 - 2 * (chan // bit % 2))
        bit *= 2
    return peer


def row_pairs(*flips):
    return [(flip, side) for flip in flips for side in (1, 0) if side or flip is not OWN]


def masks_of(chan, chans, near, far):
    is_far = chan // (chans // 2)
    return [
        2 * (a + is_far * (c - a)) + b + is_far * (d - b)
        for (a, b), (c, d) in zip(row_pairs(*near), row_pairs(*far))
    ]


def greet(peer, sem):
    pl.semaphore_signal(sem, inc=1, device_id={"chan": peer}, device_id_type=MESH)


def is_swap(chans, width, tokens):
    return chans == 8 and width == BLOCK and tokens == chans * BLOCK


def split_of(groups):
    return 2 if groups % 2 == 0 else 1


def halves(end):
    bits = []
    while end > 1:
        end //= 2
        bits.append(end)
    return bits


def fused(
    ctx,
    chans,
    proj_in,
    taps_in,
    rate_in,
    residue_in,
    skip_in,
    weight_ref,
    out_ref,
    proj_ref,
    taps_ref,
    rate_ref,
    residue_ref,
    skip_ref,
    halo,
    query,
    mixed,
    work,
    bands,
    tall,
    rate_s,
    residue_s,
    powers,
    across,
    inner,
    own_end,
    ends,
    own_weight,
    gath,
    weight_sem,
    load_sems,
    halo_sems,
    end_send,
    end_recv,
    meet_sems,
    *rest,
):
    width, tokens = proj_ref.shape[1:]
    modes = rate_ref.shape[0]
    groups, blocks = width // GROUP, tokens // BLOCK
    lanes = blocks * GROUP
    split = split_of(groups)
    per, span, half = groups // split, BLOCK // split, width // split
    planes = own_end.shape[1] // groups
    swap = is_swap(chans, width, tokens)
    index = lax.axis_index("ctx")
    chan = lax.axis_index("chan")
    if swap:
        row, last_row = chan // 2, chans // 2 - 1
        peers = [(chan + 1 - 2 * (chan % 2), None), (chan - 2, row > 0), (chan + 2, row < last_row)]
        parts, turned_weight, results, there_send, there_recv, back_send, back_recv = rest
    else:
        place = ring_place(chan, chans)
        right = ring_chan((place + 1) % chans, chans)
        left = ring_chan((place + chans - 1) % chans, chans)
        peers = [(left, None), (right, None)]

    barrier = pltpu.get_barrier_semaphore()
    for hop in range(1, ctx):
        pl.semaphore_signal(
            barrier, inc=1, device_id={"ctx": (index + hop) % ctx}, device_id_type=MESH
        )
    expected = ctx - 1
    for peer, there_is in peers:
        if there_is is None:
            greet(peer, barrier)
            expected = expected + 1
        else:
            pl.when(there_is)(functools.partial(greet, peer, barrier))
            expected = expected + jnp.where(there_is, 1, 0)

    loads = [
        pltpu.make_async_copy(source, target, load_sems.at[k])
        for k, (source, target) in enumerate(
            (
                (taps_in, taps_ref),
                (rate_in, rate_ref),
                (residue_in, residue_ref),
                (skip_in, skip_ref),
                (proj_in, proj_ref),
            )
        )
    ]
    for load in loads:
        load.start()
    if swap or weight_ref.shape[1] == width:
        weight_from = weight_ref
    else:
        weight_from = weight_ref.at[:, pl.ds(pl.multiple_of(chan * width, width), width)]
    weight_copy = pltpu.make_async_copy(weight_from, own_weight, weight_sem)

    loads[0].wait()
    all_groups = taps_ref.shape[1]
    pick = one_hot(
        iota((groups, all_groups), 1) == iota((groups, all_groups), 0) + chan * groups,
        jnp.bfloat16,
    )
    flip = one_hot(
        iota((BLOCK, 2 * BLOCK), 1) == BLOCK - iota((BLOCK, 2 * BLOCK), 0), jnp.bfloat16
    )

    def make_bands(stream):
        own = jnp.dot(pick, taps_ref[stream], preferred_element_type=jnp.float32)
        rows = jnp.dot(own.astype(jnp.bfloat16), flip, preferred_element_type=jnp.float32)
        for g in range(groups):
            wide = jnp.broadcast_to(rows[g : g + 1, :], (BLOCK, 2 * BLOCK))
            bands[stream, g] = pltpu.roll(wide, 0, 1, stride=1, stride_axis=0).astype(
                jnp.bfloat16
            )

    make_bands(1)
    make_bands(2)

    loads[4].wait()
    pl.semaphore_wait(barrier, expected)
    halo_parts = [(pl.ds(1, 2), pl.ds(p * half, half)) for p in range(split)]
    halo_parts.append((pl.ds(0, 1), pl.ds(0, width)))
    halo_copies = [
        pltpu.make_async_remote_copy(
            src_ref=proj_ref.at[streams, rows, pl.ds(tokens - BLOCK, BLOCK)],
            dst_ref=halo.at[streams, rows],
            send_sem=halo_sems.at[2 * k],
            recv_sem=halo_sems.at[2 * k + 1],
            device_id={"ctx": (index + 1) % ctx},
            device_id_type=MESH,
        )
        for k, (streams, rows) in enumerate(halo_parts)
    ]

    @pl.when(index < ctx - 1)
    def _():
        for copy in halo_copies:
            copy.start()

    @pl.when(index == 0)
    def _():
        halo[...] = jnp.zeros_like(halo)

    weight_copy.start()

    if swap:
        up, down = meet_sems.at[0], meet_sems.at[1]

        @pl.when(row == 0)
        def _():
            greet(chan + 2, up)

        @pl.when(row == last_row)
        def _():
            greet(chan - 2, down)

        def pass_down():
            pl.semaphore_wait(down, 1)

            @pl.when(row > 0)
            def _():
                greet(chan - 2, down)

    shape = (groups, lanes)
    tile_at = iota(shape, 1) // GROUP
    part_at = iota(shape, 0) // per
    tile_axis, part_axis = (tile_at, GROUP, 1, blocks), (part_at, per, 0, split)
    spread = one_hot(iota((width, lanes), 0) % GROUP == iota((width, lanes), 1) % GROUP)

    def mode_rows(m):
        return slice(m * groups, (m + 1) * groups)

    def entry_rows(p, m):
        return pl.ds((p * modes + m) * groups, groups)

    own_group = iota((groups, width), 1) // GROUP == iota((groups, width), 0)

    def spread_rows(rows):
        for m, row_of in enumerate(rows):
            tall[mode_rows(m), :] = jnp.where(
                own_group, jnp.broadcast_to(row_of, (groups, width)), 0.0
            )
        return jnp.dot(
            tall[0 : len(rows) * groups, :],
            spread,
            precision=HIGHEST,
            preferred_element_type=jnp.float32,
        )

    def moved_to(value, p, part):
        shift = (part - p) * per % groups
        return pltpu.roll(value, shift, 0) if shift else value

    def of_piece(value, p):
        whole = moved_to(value, p, 0)
        for part in range(1, split):
            whole = jnp.where(part_at == part, moved_to(value, p, part), whole)
        return whole

    def slot_of(m):
        return m // (blocks * split), m // blocks % split, m % blocks

    def gathered(values, axis_of):
        at, size, axis, count = axis_of
        full = shape[axis]
        for bit in halves(count):
            low = at // bit % 2 == 0
            merged = []
            for first, second in zip(values[:bit], values[bit:]):
                kept, moving = jnp.where(low, first, second), jnp.where(low, second, first)
                up = pltpu.roll(moving, size * bit, axis)
                if 2 * bit != count:
                    up = jnp.where(low, pltpu.roll(moving, full - size * bit, axis), up)
                merged.append(kept + up)
            values = merged
        return values[0]

    def spread_out(value, axis_of):
        at, size, axis, count = axis_of
        values = [value]
        for bit in halves(count):
            low = at // bit % 2 == 0
            moved = [pltpu.roll(v, size * bit, axis) for v in values]
            pairs = [
                (jnp.where(low, v, r), jnp.where(low, r, v)) for v, r in zip(values, moved)
            ]
            values = [v for pair in pairs for v in pair]
        return values

    loads[1].wait()
    rate_s[...] = spread_rows([rate_ref[m : m + 1, :] for m in range(modes)])
    at_end = (BLOCK * (blocks - 1 - tile_at) + span * (split - 1 - part_at)).astype(jnp.float32)
    at_start = (BLOCK * tile_at + span * part_at).astype(jnp.float32)
    for m in range(modes):
        rates = rate_s[mode_rows(m), :]
        decay, far_decay = jnp.exp(-rates), jnp.exp(rates * (-float(span)))
        for p in range(split):
            own_rates = of_piece(rates, p)
            powers[0, entry_rows(p, m), :] = of_piece(decay, p)
            powers[1, entry_rows(p, m), :] = of_piece(far_decay, p)
            powers[2, entry_rows(p, m), :] = jnp.exp(-own_rates * at_start)
            powers[3, entry_rows(p, m), :] = jnp.exp(-own_rates * at_end)

    make_bands(0)
    loads[2].wait()
    loads[3].wait()
    weights = spread_rows([residue_ref[m : m + 1, :] for m in range(modes)])
    residue_s[0 : modes * groups, :] = weights * jnp.sqrt(2.0 * rate_s[...] / modes)
    residue_s[modes * groups : (modes + 1) * groups, :] = spread_rows([skip_ref[...]])
    for m in range(modes):
        for p in range(split):
            powers[4, entry_rows(p, m), :] = of_piece(residue_s[mode_rows(m), :], p)

    def late_tables():
        packed = {}
        for m in range(modes):
            rates = rate_s[mode_rows(m), :]
            plane, part, tile = slot_of(m)
            packed[plane, part] = jnp.where(tile_at == tile, rates, packed.get((plane, part), rates))
        for p in range(split):
            for plane in range(planes):
                whole = jnp.zeros(shape, jnp.float32)
                for part in range(split):
                    if (plane, part) in packed:
                        placed = moved_to(packed[plane, part], p, part)
                        whole = jnp.where(part_at == part, placed, whole)
                across[p, plane * groups : (plane + 1) * groups, :] = jnp.exp(
                    whole * (-float(tokens))
                )

    late_tables()

    def short(stream, g):
        rows_of = slice(g * GROUP, (g + 1) * GROUP)
        tiles = [proj_ref[stream, rows_of, b * BLOCK : (b + 1) * BLOCK] for b in range(blocks)]
        before = [halo[stream, rows_of, :]] + tiles[:-1]
        signal = jnp.concatenate(
            [jnp.concatenate(before, axis=0), jnp.concatenate(tiles, axis=0)], axis=1
        )
        return lax.dot_general(
            bands[stream, g], signal, (((1,), (1,)), ((), ())), preferred_element_type=jnp.float32
        )

    def strided(p, part, inside):
        return pl.ds(p * span * groups + part * per + inside, span, stride=groups)

    def keep(ref, g, value):
        p, inside = g // per, g % per
        for part in range(split):
            ref[strided(p, part, inside), :] = value[part * span : (part + 1) * span]

    def step_rows(p, r):
        return pl.ds(pl.multiple_of((p * span + r) * groups, groups), groups)

    def power(k, p, m):
        return powers[k, entry_rows(p, m), :]

    zero = jnp.zeros(shape, jnp.float32)

    def end_copy(hop, p):
        return pltpu.make_async_remote_copy(
            src_ref=own_end.at[p],
            dst_ref=ends.at[hop - 1, p],
            send_sem=end_send.at[hop - 1, p],
            recv_sem=end_recv.at[hop - 1, p],
            device_id={"ctx": (index + hop) % ctx},
            device_id_type=MESH,
        )

    end_copies = {(hop, p): end_copy(hop, p) for hop in range(1, ctx) for p in range(split)}

    def first_pass(p):
        @pl.when(index > 0)
        def _():
            halo_copies[p].wait_recv()

        for g in range(p * per, (p + 1) * per):
            keep(mixed, g, short(1, g) * short(2, g))
        decay = [power(0, p, m) for m in range(modes)]

        def gather_step(r, states):
            x = mixed[step_rows(p, r), :]
            return tuple(d * s + x for d, s in zip(decay, states))

        last = lax.fori_loop(0, span, gather_step, (zero,) * modes, unroll=16)
        for plane in range(planes):
            by_part = []
            for part in range(split):
                first = (plane * split + part) * blocks
                ending = [
                    last[m] * power(3, p, m) if m < modes else zero
                    for m in range(first, first + blocks)
                ]
                by_part.append(gathered(ending, tile_axis))
            own_end[p, plane * groups : (plane + 1) * groups, :] = gathered(by_part, part_axis)
        for hop in range(1, ctx):

            @pl.when(index < ctx - hop)
            def _():
                end_copies[hop, p].start()

        for m in range(modes):
            inner[entry_rows(p, m), :] = last[m]

    def second_pass(p):
        for g in range(p * per, (p + 1) * per):
            keep(query, g, short(0, g))
        for m in range(modes):
            total = inner[entry_rows(p, m), :]
            far_decay = tile_decay = power(1, p, m)
            if split > 1:
                other = pltpu.roll(total, per, 0)
                inside = jnp.where(part_at == 1, other, 0.0)
                total = jnp.where(
                    part_at == 0, far_decay * total + other, far_decay * other + total
                )
                tile_decay = far_decay * far_decay
            before, factor = zero, None
            for hop in range(1, min(4, blocks) + 1):
                moved = jnp.where(tile_at >= hop, pltpu.roll(total, GROUP * hop % lanes, 1), 0.0)
                before = before + (moved if factor is None else factor * moved)
                factor = tile_decay if factor is None else factor * tile_decay
            hop = 4
            while hop < blocks:
                moved = jnp.where(tile_at >= hop, pltpu.roll(before, GROUP * hop, 1), 0.0)
                before = before + factor * moved
                factor = factor * factor
                hop *= 2
            if split > 1:
                before = jnp.where(part_at == 1, far_decay, 1.0) * before + inside
            inner[entry_rows(p, m), :] = before
        for hop in range(1, ctx):

            @pl.when(index >= hop)
            def _():
                end_copies[hop, p].wait_recv()

            @pl.when(index < hop)
            def _():
                ends[hop - 1, p] = jnp.zeros(ends.shape[2:], jnp.float32)

        arrived = []
        for plane in range(planes):
            rows = slice(plane * groups, (plane + 1) * groups)
            total = zero
            for hop in range(ctx - 1, 0, -1):
                total = across[p, rows, :] * total + ends[hop - 1, p, rows, :]
            arrived.append(total)
        incoming = [
            value
            for total in arrived
            for by_part in spread_out(total, part_axis)
            for value in spread_out(by_part, tile_axis)
        ]
        entry = [
            inner[entry_rows(p, m), :] + power(2, p, m) * incoming[m] for m in range(modes)
        ]
        decay = [power(0, p, m) for m in range(modes)]
        weight = [power(4, p, m) for m in range(modes)]
        skip = of_piece(residue_s[mode_rows(modes), :], p)

        def step(r, states):
            where = step_rows(p, r)
            x = mixed[where, :]
            new = tuple(d * s + x for d, s in zip(decay, states))
            terms = [w * s for w, s in zip(weight, new)] + [skip * x]
            while len(terms) > 1:
                terms = [a + b for a, b in zip(terms[::2], terms[1::2])] + (
                    [terms[-1]] if len(terms) % 2 else []
                )
            work[where, :] = query[where, :] * terms[0]
            return new

        lax.fori_loop(0, span, step, tuple(entry), unroll=8)

    def turn(p, put):
        for inside in range(per):
            rows = [work[strided(p, part, inside), :] for part in range(split)]
            whole = jnp.concatenate(rows, axis=0) if split > 1 else rows[0]
            turned = whole.astype(jnp.bfloat16).T
            for b in range(blocks):
                put(p * per + inside, b, turned[b * GROUP : (b + 1) * GROUP])

    for p in range(split):
        first_pass(p)
    if swap:

        @pl.when(row > 0)
        def _():
            pl.semaphore_wait(up, 1)

        @pl.when(jnp.logical_and(row > 0, row < last_row))
        def _():
            greet(chan + 2, up)

        pl.when(jnp.logical_and(row > last_row // 2, row < last_row))(pass_down)

    @pl.when(index > 0)
    def _():
        halo_copies[split].wait_recv()

    if swap:
        there = []

        def put(g, b, tile):
            parts[b, g * GROUP : (g + 1) * GROUP, :] = tile

        for p in range(split):
            second_pass(p)
            turn(p, put)
            if p == 0:
                pl.when(row <= last_row // 2)(pass_down)
            rows = pl.ds(p * half, half)
            beside = row + 1 - 2 * (row % 2)
            for mask in masks_of(chan, chans, (3, 2, 1, OWN), (1, OWN, row, beside)):
                peer = flipped_by(chan, chans, mask)
                there.append(
                    pltpu.make_async_remote_copy(
                        src_ref=parts.at[peer, rows],
                        dst_ref=gath.at[chan, rows],
                        send_sem=there_send.at[p, mask - 1],
                        recv_sem=there_recv.at[p, mask - 1],
                        device_id={"chan": peer},
                        device_id_type=MESH,
                    )
                )
                there[-1].start()
        exchange(
            chans,
            chan,
            gath,
            own_weight,
            weight_copy,
            out_ref,
            parts,
            turned_weight,
            results,
            there,
            back_send,
            back_recv,
        )
    else:
        per_piece = blocks // PIECES

        def put(g, b, tile):
            inside = (b % per_piece) * BLOCK
            gath[
                chan, b // per_piece, g * GROUP : (g + 1) * GROUP, inside : inside + BLOCK
            ] = tile

        for p in range(split):
            second_pass(p)
            turn(p, put)
        ring(chans, chan, place, left, right, gath, own_weight, weight_copy, out_ref, *rest)

    @pl.when(index < ctx - 1)
    def _():
        for copy in halo_copies:
            copy.wait_send()

    for hop in range(1, ctx):

        @pl.when(index < ctx - hop)
        def _():
            for p in range(split):
                end_copies[hop, p].wait_send()


def per_device(ctx, chans, proj, taps, rate, residue, skip, out_weight):
    width, tokens = proj.shape[1:]
    modes = rate.shape[1]
    groups, blocks = width // GROUP, tokens // BLOCK
    lanes = blocks * GROUP
    split = split_of(groups)
    planes = -(-modes // (blocks * split))
    swap = is_swap(chans, width, tokens)
    if width % 128:
        out_weight = lax.dynamic_slice_in_dim(
            out_weight, lax.axis_index("chan") * width, width, 1
        )
    vmem = pl.BlockSpec(memory_space=pltpu.VMEM)
    if swap:
        blocks_of = pltpu.VMEM((chans, width, BLOCK), jnp.bfloat16)
        square = pltpu.VMEM(out_weight.shape, jnp.bfloat16)
        several = pltpu.SemaphoreType.DMA((chans - 1,))
        by_part = pltpu.SemaphoreType.DMA((split, chans - 1))
        weight_scratch, gath_scratch = square, blocks_of
        rest = [blocks_of, square, blocks_of, by_part, by_part, several, several]
    else:
        weight_scratch = pltpu.VMEM((chans * width, width), jnp.bfloat16)
        gath_scratch = pltpu.VMEM((chans, PIECES, width, tokens // PIECES), jnp.bfloat16)
        hops = pltpu.SemaphoreType.DMA((2, chans // 2, PIECES))
        rest = [pltpu.VMEM((PIECES, width, tokens // PIECES), jnp.float32), hops, hops]
    major = pltpu.VMEM((BLOCK * groups, lanes), jnp.float32)
    rows = split * modes * groups
    table = pltpu.VMEM((rows, lanes), jnp.float32)
    packed = (split, planes * groups, lanes)
    return pl.pallas_call(
        functools.partial(fused, ctx, chans),
        out_shape=pltpu.VMEM((width, tokens), jnp.bfloat16),
        in_specs=[pl.BlockSpec(memory_space=pltpu.HBM)] * 6,
        out_specs=vmem,
        scratch_shapes=[
            pltpu.VMEM(proj.shape, proj.dtype),
            pltpu.VMEM(taps.shape, taps.dtype),
            pltpu.VMEM((modes, width), jnp.float32),
            pltpu.VMEM((modes, width), jnp.float32),
            pltpu.VMEM((1, width), jnp.float32),
            pltpu.VMEM((3, width, BLOCK), jnp.bfloat16),
            major,
            major,
            major,
            pltpu.VMEM((3, groups, BLOCK, 2 * BLOCK), jnp.bfloat16),
            pltpu.VMEM((modes * groups, width), jnp.float32),
            pltpu.VMEM((modes * groups, lanes), jnp.float32),
            pltpu.VMEM(((modes + 1) * groups, lanes), jnp.float32),
            pltpu.VMEM((5, rows, lanes), jnp.float32),
            pltpu.VMEM(packed, jnp.float32),
            table,
            pltpu.VMEM(packed, jnp.float32),
            pltpu.VMEM((ctx - 1, *packed), jnp.float32),
            weight_scratch,
            gath_scratch,
            pltpu.SemaphoreType.DMA,
            pltpu.SemaphoreType.DMA((5,)),
            pltpu.SemaphoreType.DMA((2 * (split + 1),)),
            pltpu.SemaphoreType.DMA((ctx - 1, split)),
            pltpu.SemaphoreType.DMA((ctx - 1, split)),
            pltpu.SemaphoreType.REGULAR((2,)),
            *rest,
        ],
        compiler_params=pltpu.CompilerParams(
            vmem_limit_bytes=58 << 20, collective_id=0, has_side_effects=True
        ),
        name="fused",
    )(proj, taps, rate.T, residue.T, skip.reshape(1, width), out_weight)


def solution(mesh):
    in_specs = (P(None, "chan", "ctx"), P(), P("chan", None), P("chan", None), P("chan"), P())
    out_specs = P("chan", "ctx")
    return jax.shard_map(
        functools.partial(per_device, mesh.shape["ctx"], mesh.shape["chan"]),
        mesh=mesh,
        in_specs=in_specs,
        out_specs=out_specs,
        check_vma=False,
    )
```

```python
import functools
import jax
import jax.numpy as jnp
from jax import lax
from jax.experimental import pallas as pl
from jax.experimental.pallas import tpu as pltpu
from jax.sharding import PartitionSpec as P

GROUP = 16
BLOCK = 128
PIECES = 4
OWN = 0
MESH = pl.DeviceIdType.MESH
HIGHEST = lax.Precision.HIGHEST


def iota(shape, axis):
    return lax.broadcasted_iota(jnp.int32, shape, axis)


def one_hot(hit, dtype=jnp.float32):
    return hit.astype(jnp.float32).astype(dtype)


def ring_place(chan, n):
    row, side = chan // 2, chan % 2
    return row + side * (n - 1 - 2 * row)


def ring_chan(place, n):
    side = place // (n // 2)
    row = place + side * (n - 1 - 2 * place)
    return 2 * row + side


def exchange(
    chans,
    chan,
    gath,
    weight,
    weight_copy,
    out_ref,
    parts,
    turned_weight,
    results,
    there,
    back_send,
    back_recv,
):
    width = out_ref.shape[0]
    gath[chan] = parts[chan]
    weight_copy.wait()
    turned_weight[...] = weight[...].T
    for copy in there:
        copy.wait_recv()
    everything = gath[...].reshape(chans * width, BLOCK)

    def project(shard):
        rows_of = pl.ds(pl.multiple_of(shard * width, width), width)
        return jnp.dot(
            turned_weight[rows_of, :], everything, preferred_element_type=jnp.float32
        ).astype(jnp.bfloat16)

    own_columns = pl.ds(pl.multiple_of(chan * BLOCK, BLOCK), BLOCK)
    back = []
    row = chan // 2
    beside = row + 1 - 2 * (row % 2)
    for mask in masks_of(chan, chans, (1, OWN, 3, 2), (row, 1, OWN, beside)):
        peer = flipped_by(chan, chans, mask)
        if len(back) >= 5:
            pl.when(lax.axis_index("ctx") % 2 == 1)(back[len(back) - 5].wait_send)
        results[mask - 1] = project(peer)
        back.append(
            pltpu.make_async_remote_copy(
                src_ref=results.at[mask - 1],
                dst_ref=out_ref.at[:, own_columns],
                send_sem=back_send.at[mask - 1],
                recv_sem=back_recv.at[mask - 1],
                device_id={"chan": peer},
                device_id_type=MESH,
            )
        )
        back[-1].start()
    out_ref[:, own_columns] = project(chan)
    for copy in back:
        copy.wait_recv()
    for copy in there + back[2:]:
        copy.wait_send()
    for copy in back[:2]:
        pl.when(lax.axis_index("ctx") % 2 != 1)(copy.wait_send)


def ring(
    chans,
    chan,
    place,
    left,
    right,
    gath,
    own_weight,
    weight_copy,
    out_ref,
    acc,
    ring_send,
    ring_recv,
):
    width, tokens = out_ref.shape
    cols = tokens // PIECES
    half = chans // 2

    def ring_copy(way, hop, piece):
        shard = ring_chan((place + chans + (-hop if way == 0 else hop)) % chans, chans)
        return pltpu.make_async_remote_copy(
            src_ref=gath.at[shard, piece],
            dst_ref=gath.at[shard, piece],
            send_sem=ring_send.at[way, hop, piece],
            recv_sem=ring_recv.at[way, hop, piece],
            device_id={"chan": right if way == 0 else left},
            device_id_type=MESH,
        )

    def travels(way, hop, piece):
        if hop < half - 1:
            return True
        return hop == half - 1 and (piece < PIECES // 2) == (way == 0)

    copies = {}
    for piece in range(PIECES):
        for way in range(2):
            copies[way, 0, piece] = ring_copy(way, 0, piece)
            copies[way, 0, piece].start()
    weight_copy.wait()

    def project(shard, piece):
        rows_of = pl.ds(pl.multiple_of(shard * width, width), width)
        return lax.dot_general(
            own_weight[rows_of, :],
            gath[shard, piece],
            (((0,), (0,)), ((), ())),
            preferred_element_type=jnp.float32,
        )

    for piece in range(PIECES):
        acc[piece] = project(chan, piece)
    for hop in range(1, half + 1):
        for piece in range(PIECES):
            arrived = []
            for way in range(2):
                if not travels(way, hop - 1, piece):
                    continue
                copies[way, hop - 1, piece].wait_recv()
                if travels(way, hop, piece):
                    copies[way, hop, piece] = ring_copy(way, hop, piece)
                    copies[way, hop, piece].start()
                arrived.append(
                    ring_chan((place + chans + (-hop if way == 0 else hop)) % chans, chans)
                )
            total = acc[piece]
            for shard in arrived:
                total = total + project(shard, piece)
            if hop == half:
                out_ref[:, piece * cols : (piece + 1) * cols] = total.astype(out_ref.dtype)
            else:
                acc[piece] = total

    for key in copies:
        copies[key].wait_send()


def flipped_by(chan, chans, mask):
    peer, bit = chan, 1
    while bit < chans:
        peer = peer + bit * (mask // bit % 2) * (1 - 2 * (chan // bit % 2))
        bit *= 2
    return peer


def row_pairs(*flips):
    return [(flip, side) for flip in flips for side in (1, 0) if side or flip is not OWN]


def masks_of(chan, chans, near, far):
    is_far = chan // (chans // 2)
    return [
        2 * (a + is_far * (c - a)) + b + is_far * (d - b)
        for (a, b), (c, d) in zip(row_pairs(*near), row_pairs(*far))
    ]


def greet(peer, sem):
    pl.semaphore_signal(sem, inc=1, device_id={"chan": peer}, device_id_type=MESH)


def is_swap(chans, width, tokens):
    return chans == 8 and width == BLOCK and tokens == chans * BLOCK


def split_of(groups):
    return 2 if groups % 2 == 0 else 1


def halves(end):
    bits = []
    while end > 1:
        end //= 2
        bits.append(end)
    return bits


def fused(
    ctx,
    chans,
    proj_in,
    taps_in,
    rate_in,
    residue_in,
    skip_in,
    weight_ref,
    out_ref,
    proj_ref,
    taps_ref,
    rate_ref,
    residue_ref,
    skip_ref,
    halo,
    query,
    mixed,
    work,
    bands,
    tall,
    rate_s,
    residue_s,
    powers,
    across,
    inner,
    own_end,
    ends,
    own_weight,
    gath,
    weight_sem,
    load_sems,
    halo_sems,
    end_send,
    end_recv,
    meet_sems,
    *rest,
):
    width, tokens = proj_ref.shape[1:]
    modes = rate_ref.shape[0]
    groups, blocks = width // GROUP, tokens // BLOCK
    lanes = blocks * GROUP
    split = split_of(groups)
    per, span, half = groups // split, BLOCK // split, width // split
    planes = own_end.shape[1] // groups
    swap = is_swap(chans, width, tokens)
    index = lax.axis_index("ctx")
    chan = lax.axis_index("chan")
    if swap:
        row, last_row = chan // 2, chans // 2 - 1
        peers = [(chan + 1 - 2 * (chan % 2), None), (chan - 2, row > 0), (chan + 2, row < last_row)]
        parts, turned_weight, results, there_send, there_recv, back_send, back_recv = rest
    else:
        place = ring_place(chan, chans)
        right = ring_chan((place + 1) % chans, chans)
        left = ring_chan((place + chans - 1) % chans, chans)
        peers = [(left, None), (right, None)]

    barrier = pltpu.get_barrier_semaphore()
    for hop in range(1, ctx):
        pl.semaphore_signal(
            barrier, inc=1, device_id={"ctx": (index + hop) % ctx}, device_id_type=MESH
        )
    expected = ctx - 1
    for peer, there_is in peers:
        if there_is is None:
            greet(peer, barrier)
            expected = expected + 1
        else:
            pl.when(there_is)(functools.partial(greet, peer, barrier))
            expected = expected + jnp.where(there_is, 1, 0)

    loads = [
        pltpu.make_async_copy(source, target, load_sems.at[k])
        for k, (source, target) in enumerate(
            (
                (taps_in, taps_ref),
                (rate_in, rate_ref),
                (residue_in, residue_ref),
                (skip_in, skip_ref),
                (proj_in, proj_ref),
            )
        )
    ]
    for load in loads:
        load.start()
    if swap or weight_ref.shape[1] == width:
        weight_from = weight_ref
    else:
        weight_from = weight_ref.at[:, pl.ds(pl.multiple_of(chan * width, width), width)]
    weight_copy = pltpu.make_async_copy(weight_from, own_weight, weight_sem)

    loads[0].wait()
    all_groups = taps_ref.shape[1]
    pick = one_hot(
        iota((groups, all_groups), 1) == iota((groups, all_groups), 0) + chan * groups,
        jnp.bfloat16,
    )
    flip = one_hot(
        iota((BLOCK, 2 * BLOCK), 1) == BLOCK - iota((BLOCK, 2 * BLOCK), 0), jnp.bfloat16
    )

    def make_bands(stream):
        own = jnp.dot(pick, taps_ref[stream], preferred_element_type=jnp.float32)
        rows = jnp.dot(own.astype(jnp.bfloat16), flip, preferred_element_type=jnp.float32)
        for g in range(groups):
            wide = jnp.broadcast_to(rows[g : g + 1, :], (BLOCK, 2 * BLOCK))
            bands[stream, g] = pltpu.roll(wide, 0, 1, stride=1, stride_axis=0).astype(
                jnp.bfloat16
            )

    make_bands(1)
    make_bands(2)

    loads[4].wait()
    pl.semaphore_wait(barrier, expected)
    halo_parts = [(pl.ds(1, 2), pl.ds(p * half, half)) for p in range(split)]
    halo_parts.append((pl.ds(0, 1), pl.ds(0, width)))
    halo_copies = [
        pltpu.make_async_remote_copy(
            src_ref=proj_ref.at[streams, rows, pl.ds(tokens - BLOCK, BLOCK)],
            dst_ref=halo.at[streams, rows],
            send_sem=halo_sems.at[2 * k],
            recv_sem=halo_sems.at[2 * k + 1],
            device_id={"ctx": (index + 1) % ctx},
            device_id_type=MESH,
        )
        for k, (streams, rows) in enumerate(halo_parts)
    ]

    @pl.when(index < ctx - 1)
    def _():
        for copy in halo_copies:
            copy.start()

    @pl.when(index == 0)
    def _():
        halo[...] = jnp.zeros_like(halo)

    weight_copy.start()

    if swap:
        up, down = meet_sems.at[0], meet_sems.at[1]

        @pl.when(row == 0)
        def _():
            greet(chan + 2, up)

        @pl.when(row == last_row)
        def _():
            greet(chan - 2, down)

        def pass_down():
            pl.semaphore_wait(down, 1)

            @pl.when(row > 0)
            def _():
                greet(chan - 2, down)

    shape = (groups, lanes)
    tile_at = iota(shape, 1) // GROUP
    part_at = iota(shape, 0) // per
    tile_axis, part_axis = (tile_at, GROUP, 1, blocks), (part_at, per, 0, split)
    spread = one_hot(iota((width, lanes), 0) % GROUP == iota((width, lanes), 1) % GROUP)

    def mode_rows(m):
        return slice(m * groups, (m + 1) * groups)

    def entry_rows(p, m):
        return pl.ds((p * modes + m) * groups, groups)

    own_group = iota((groups, width), 1) // GROUP == iota((groups, width), 0)

    def spread_rows(rows):
        for m, row_of in enumerate(rows):
            tall[mode_rows(m), :] = jnp.where(
                own_group, jnp.broadcast_to(row_of, (groups, width)), 0.0
            )
        return jnp.dot(
            tall[0 : len(rows) * groups, :],
            spread,
            precision=HIGHEST,
            preferred_element_type=jnp.float32,
        )

    def moved_to(value, p, part):
        shift = (part - p) * per % groups
        return pltpu.roll(value, shift, 0) if shift else value

    def of_piece(value, p):
        whole = moved_to(value, p, 0)
        for part in range(1, split):
            whole = jnp.where(part_at == part, moved_to(value, p, part), whole)
        return whole

    def slot_of(m):
        return m // (blocks * split), m // blocks % split, m % blocks

    def gathered(values, axis_of):
        at, size, axis, count = axis_of
        full = shape[axis]
        for bit in halves(count):
            low = at // bit % 2 == 0
            merged = []
            for first, second in zip(values[:bit], values[bit:]):
                kept, moving = jnp.where(low, first, second), jnp.where(low, second, first)
                up = pltpu.roll(moving, size * bit, axis)
                if 2 * bit != count:
                    up = jnp.where(low, pltpu.roll(moving, full - size * bit, axis), up)
                merged.append(kept + up)
            values = merged
        return values[0]

    def spread_out(value, axis_of):
        at, size, axis, count = axis_of
        values = [value]
        for bit in halves(count):
            low = at // bit % 2 == 0
            moved = [pltpu.roll(v, size * bit, axis) for v in values]
            pairs = [
                (jnp.where(low, v, r), jnp.where(low, r, v)) for v, r in zip(values, moved)
            ]
            values = [v for pair in pairs for v in pair]
        return values

    loads[1].wait()
    rate_s[...] = spread_rows([rate_ref[m : m + 1, :] for m in range(modes)])
    at_end = (BLOCK * (blocks - 1 - tile_at) + span * (split - 1 - part_at)).astype(jnp.float32)
    at_start = (BLOCK * tile_at + span * part_at).astype(jnp.float32)
    for m in range(modes):
        rates = rate_s[mode_rows(m), :]
        decay, far_decay = jnp.exp(-rates), jnp.exp(rates * (-float(span)))
        for p in range(split):
            own_rates = of_piece(rates, p)
            powers[0, entry_rows(p, m), :] = of_piece(decay, p)
            powers[1, entry_rows(p, m), :] = of_piece(far_decay, p)
            powers[2, entry_rows(p, m), :] = jnp.exp(-own_rates * at_start)
            powers[3, entry_rows(p, m), :] = jnp.exp(-own_rates * at_end)

    make_bands(0)
    loads[2].wait()
    loads[3].wait()
    weights = spread_rows([residue_ref[m : m + 1, :] for m in range(modes)])
    residue_s[0 : modes * groups, :] = weights * jnp.sqrt(2.0 * rate_s[...] / modes)
    residue_s[modes * groups : (modes + 1) * groups, :] = spread_rows([skip_ref[...]])
    for m in range(modes):
        for p in range(split):
            powers[4, entry_rows(p, m), :] = of_piece(residue_s[mode_rows(m), :], p)

    def late_tables():
        packed = {}
        for m in range(modes):
            rates = rate_s[mode_rows(m), :]
            plane, part, tile = slot_of(m)
            packed[plane, part] = jnp.where(tile_at == tile, rates, packed.get((plane, part), rates))
        for p in range(split):
            for plane in range(planes):
                whole = jnp.zeros(shape, jnp.float32)
                for part in range(split):
                    if (plane, part) in packed:
                        placed = moved_to(packed[plane, part], p, part)
                        whole = jnp.where(part_at == part, placed, whole)
                across[p, plane * groups : (plane + 1) * groups, :] = jnp.exp(
                    whole * (-float(tokens))
                )

    late_tables()

    def short(stream, g):
        rows_of = slice(g * GROUP, (g + 1) * GROUP)
        tiles = [proj_ref[stream, rows_of, b * BLOCK : (b + 1) * BLOCK] for b in range(blocks)]
        before = [halo[stream, rows_of, :]] + tiles[:-1]
        signal = jnp.concatenate(
            [jnp.concatenate(before, axis=0), jnp.concatenate(tiles, axis=0)], axis=1
        )
        return lax.dot_general(
            bands[stream, g], signal, (((1,), (1,)), ((), ())), preferred_element_type=jnp.float32
        )

    def strided(p, part, inside):
        return pl.ds(p * span * groups + part * per + inside, span, stride=groups)

    def keep(ref, g, value):
        p, inside = g // per, g % per
        for part in range(split):
            ref[strided(p, part, inside), :] = value[part * span : (part + 1) * span]

    def step_rows(p, r):
        return pl.ds(pl.multiple_of((p * span + r) * groups, groups), groups)

    def power(k, p, m):
        return powers[k, entry_rows(p, m), :]

    zero = jnp.zeros(shape, jnp.float32)

    def end_copy(hop, p):
        return pltpu.make_async_remote_copy(
            src_ref=own_end.at[p],
            dst_ref=ends.at[hop - 1, p],
            send_sem=end_send.at[hop - 1, p],
            recv_sem=end_recv.at[hop - 1, p],
            device_id={"ctx": (index + hop) % ctx},
            device_id_type=MESH,
        )

    end_copies = {(hop, p): end_copy(hop, p) for hop in range(1, ctx) for p in range(split)}

    def first_pass(p):
        @pl.when(index > 0)
        def _():
            halo_copies[p].wait_recv()

        for g in range(p * per, (p + 1) * per):
            keep(mixed, g, short(1, g) * short(2, g))
        decay = [power(0, p, m) for m in range(modes)]

        def gather_step(r, states):
            x = mixed[step_rows(p, r), :]
            return tuple(d * s + x for d, s in zip(decay, states))

        last = lax.fori_loop(0, span, gather_step, (zero,) * modes, unroll=16)
        for plane in range(planes):
            by_part = []
            for part in range(split):
                first = (plane * split + part) * blocks
                ending = [
                    last[m] * power(3, p, m) if m < modes else zero
                    for m in range(first, first + blocks)
                ]
                by_part.append(gathered(ending, tile_axis))
            own_end[p, plane * groups : (plane + 1) * groups, :] = gathered(by_part, part_axis)
        for hop in range(1, ctx):

            @pl.when(index < ctx - hop)
            def _():
                end_copies[hop, p].start()

        for m in range(modes):
            inner[entry_rows(p, m), :] = last[m]

    def second_pass(p):
        for g in range(p * per, (p + 1) * per):
            keep(query, g, short(0, g))
        for m in range(modes):
            total = inner[entry_rows(p, m), :]
            far_decay = tile_decay = power(1, p, m)
            if split > 1:
                other = pltpu.roll(total, per, 0)
                inside = jnp.where(part_at == 1, other, 0.0)
                total = jnp.where(
                    part_at == 0, far_decay * total + other, far_decay * other + total
                )
                tile_decay = far_decay * far_decay
            before, factor = zero, None
            for hop in range(1, min(4, blocks) + 1):
                moved = jnp.where(tile_at >= hop, pltpu.roll(total, GROUP * hop % lanes, 1), 0.0)
                before = before + (moved if factor is None else factor * moved)
                factor = tile_decay if factor is None else factor * tile_decay
            hop = 4
            while hop < blocks:
                moved = jnp.where(tile_at >= hop, pltpu.roll(before, GROUP * hop, 1), 0.0)
                before = before + factor * moved
                factor = factor * factor
                hop *= 2
            if split > 1:
                before = jnp.where(part_at == 1, far_decay, 1.0) * before + inside
            inner[entry_rows(p, m), :] = before
        for hop in range(1, ctx):

            @pl.when(index >= hop)
            def _():
                end_copies[hop, p].wait_recv()

            @pl.when(index < hop)
            def _():
                ends[hop - 1, p] = jnp.zeros(ends.shape[2:], jnp.float32)

        arrived = []
        for plane in range(planes):
            rows = slice(plane * groups, (plane + 1) * groups)
            total = zero
            for hop in range(ctx - 1, 0, -1):
                total = across[p, rows, :] * total + ends[hop - 1, p, rows, :]
            arrived.append(total)
        incoming = [
            value
            for total in arrived
            for by_part in spread_out(total, part_axis)
            for value in spread_out(by_part, tile_axis)
        ]
        entry = [
            inner[entry_rows(p, m), :] + power(2, p, m) * incoming[m] for m in range(modes)
        ]
        decay = [power(0, p, m) for m in range(modes)]
        weight = [power(4, p, m) for m in range(modes)]
        skip = of_piece(residue_s[mode_rows(modes), :], p)

        def step(r, states):
            where = step_rows(p, r)
            x = mixed[where, :]
            new = tuple(d * s + x for d, s in zip(decay, states))
            terms = [w * s for w, s in zip(weight, new)] + [skip * x]
            while len(terms) > 1:
                terms = [a + b for a, b in zip(terms[::2], terms[1::2])] + (
                    [terms[-1]] if len(terms) % 2 else []
                )
            work[where, :] = query[where, :] * terms[0]
            return new

        lax.fori_loop(0, span, step, tuple(entry), unroll=8)

    def turn(p, put):
        for inside in range(per):
            rows = [work[strided(p, part, inside), :] for part in range(split)]
            whole = jnp.concatenate(rows, axis=0) if split > 1 else rows[0]
            turned = whole.astype(jnp.bfloat16).T
            for b in range(blocks):
                put(p * per + inside, b, turned[b * GROUP : (b + 1) * GROUP])

    for p in range(split):
        first_pass(p)
    if swap:

        @pl.when(row > 0)
        def _():
            pl.semaphore_wait(up, 1)

        @pl.when(jnp.logical_and(row > 0, row < last_row))
        def _():
            greet(chan + 2, up)

        pl.when(jnp.logical_and(row > last_row // 2, row < last_row))(pass_down)

    @pl.when(index > 0)
    def _():
        halo_copies[split].wait_recv()

    if swap:
        there = []

        def put(g, b, tile):
            parts[b, g * GROUP : (g + 1) * GROUP, :] = tile

        for p in range(split):
            second_pass(p)
            turn(p, put)
            rows = pl.ds(p * half, half)
            beside = row + 1 - 2 * (row % 2)
            order = [(0, 1), (1, 0), (3, 1), (3, 0), (2, 1), (2, 0), (1, 1)]
            far_order = row_pairs(1, OWN, row, beside)
            is_far = chan // (chans // 2)
            order = [
                2 * (a + is_far * (c - a)) + b + is_far * (d - b)
                for (a, b), (c, d) in zip(order, far_order)
            ]
            for k, mask in enumerate(order):
                if p == 0 and k == 2:
                    pl.when(row <= last_row // 2)(pass_down)
                peer = flipped_by(chan, chans, mask)
                there.append(
                    pltpu.make_async_remote_copy(
                        src_ref=parts.at[peer, rows],
                        dst_ref=gath.at[chan, rows],
                        send_sem=there_send.at[p, mask - 1],
                        recv_sem=there_recv.at[p, mask - 1],
                        device_id={"chan": peer},
                        device_id_type=MESH,
                    )
                )
                there[-1].start()
        exchange(
            chans,
            chan,
            gath,
            own_weight,
            weight_copy,
            out_ref,
            parts,
            turned_weight,
            results,
            there,
            back_send,
            back_recv,
        )
    else:
        per_piece = blocks // PIECES

        def put(g, b, tile):
            inside = (b % per_piece) * BLOCK
            gath[
                chan, b // per_piece, g * GROUP : (g + 1) * GROUP, inside : inside + BLOCK
            ] = tile

        for p in range(split):
            second_pass(p)
            turn(p, put)
        ring(chans, chan, place, left, right, gath, own_weight, weight_copy, out_ref, *rest)

    @pl.when(index < ctx - 1)
    def _():
        for copy in halo_copies:
            copy.wait_send()

    for hop in range(1, ctx):

        @pl.when(index < ctx - hop)
        def _():
            for p in range(split):
                end_copies[hop, p].wait_send()


def per_device(ctx, chans, proj, taps, rate, residue, skip, out_weight):
    width, tokens = proj.shape[1:]
    modes = rate.shape[1]
    groups, blocks = width // GROUP, tokens // BLOCK
    lanes = blocks * GROUP
    split = split_of(groups)
    planes = -(-modes // (blocks * split))
    swap = is_swap(chans, width, tokens)
    if width % 128:
        out_weight = lax.dynamic_slice_in_dim(
            out_weight, lax.axis_index("chan") * width, width, 1
        )
    vmem = pl.BlockSpec(memory_space=pltpu.VMEM)
    if swap:
        blocks_of = pltpu.VMEM((chans, width, BLOCK), jnp.bfloat16)
        square = pltpu.VMEM(out_weight.shape, jnp.bfloat16)
        several = pltpu.SemaphoreType.DMA((chans - 1,))
        by_part = pltpu.SemaphoreType.DMA((split, chans - 1))
        weight_scratch, gath_scratch = square, blocks_of
        rest = [blocks_of, square, blocks_of, by_part, by_part, several, several]
    else:
        weight_scratch = pltpu.VMEM((chans * width, width), jnp.bfloat16)
        gath_scratch = pltpu.VMEM((chans, PIECES, width, tokens // PIECES), jnp.bfloat16)
        hops = pltpu.SemaphoreType.DMA((2, chans // 2, PIECES))
        rest = [pltpu.VMEM((PIECES, width, tokens // PIECES), jnp.float32), hops, hops]
    major = pltpu.VMEM((BLOCK * groups, lanes), jnp.float32)
    rows = split * modes * groups
    table = pltpu.VMEM((rows, lanes), jnp.float32)
    packed = (split, planes * groups, lanes)
    return pl.pallas_call(
        functools.partial(fused, ctx, chans),
        out_shape=pltpu.VMEM((width, tokens), jnp.bfloat16),
        in_specs=[pl.BlockSpec(memory_space=pltpu.HBM)] * 6,
        out_specs=vmem,
        scratch_shapes=[
            pltpu.VMEM(proj.shape, proj.dtype),
            pltpu.VMEM(taps.shape, taps.dtype),
            pltpu.VMEM((modes, width), jnp.float32),
            pltpu.VMEM((modes, width), jnp.float32),
            pltpu.VMEM((1, width), jnp.float32),
            pltpu.VMEM((3, width, BLOCK), jnp.bfloat16),
            major,
            major,
            major,
            pltpu.VMEM((3, groups, BLOCK, 2 * BLOCK), jnp.bfloat16),
            pltpu.VMEM((modes * groups, width), jnp.float32),
            pltpu.VMEM((modes * groups, lanes), jnp.float32),
            pltpu.VMEM(((modes + 1) * groups, lanes), jnp.float32),
            pltpu.VMEM((5, rows, lanes), jnp.float32),
            pltpu.VMEM(packed, jnp.float32),
            table,
            pltpu.VMEM(packed, jnp.float32),
            pltpu.VMEM((ctx - 1, *packed), jnp.float32),
            weight_scratch,
            gath_scratch,
            pltpu.SemaphoreType.DMA,
            pltpu.SemaphoreType.DMA((5,)),
            pltpu.SemaphoreType.DMA((2 * (split + 1),)),
            pltpu.SemaphoreType.DMA((ctx - 1, split)),
            pltpu.SemaphoreType.DMA((ctx - 1, split)),
            pltpu.SemaphoreType.REGULAR((2,)),
            *rest,
        ],
        compiler_params=pltpu.CompilerParams(
            vmem_limit_bytes=58 << 20, collective_id=0, has_side_effects=True
        ),
        name="fused",
    )(proj, taps, rate.T, residue.T, skip.reshape(1, width), out_weight)


def solution(mesh):
    in_specs = (P(None, "chan", "ctx"), P(), P("chan", None), P("chan", None), P("chan"), P())
    out_specs = P("chan", "ctx")
    return jax.shard_map(
        functools.partial(per_device, mesh.shape["ctx"], mesh.shape["chan"]),
        mesh=mesh,
        in_specs=in_specs,
        out_specs=out_specs,
        check_vma=False,
    )
```
